32 devices in a mesh: wide: 8 (over z, x), narrow: 4 (over y, core).
Axes of the slice: x: 2, y: 2, z: 4, core: 2. Of those that a mesh axis runs over, the one named last changes fastest.
Arguments:
- layer_in: bfloat16 [16, 1024, 768], P('wide', 'narrow'), may hold values from -6 to 6
- doc_ids: int32 [16, 1024], P('wide'), may hold values from 0 to 3, never falling along the last dimension, each value on 1 to 512 neighbouring positions
- in_proj: bfloat16 [3, 768, 768], P(None, ('wide', 'narrow')), may hold values from -0.21875 to 0.21875
- out_proj: bfloat16 [768, 768], P(('wide', 'narrow')), may hold values from -1.75 to 1.75
- vec_bias: bfloat16 [6, 768], P(None, ('wide', 'narrow')), may hold values from -3 to 3
- norm_gain: bfloat16 [2, 768], P(None, ('wide', 'narrow')), may hold values from 0.5 to 1.5
- ffn_in: bfloat16 [768, 3072], P(('wide', 'narrow')), may hold values from -0.21875 to 0.21875
- ffn_bias: bfloat16 [3072], P(('wide', 'narrow')), may hold values from -3 to 3
- ffn_out: bfloat16 [3072, 768], P(('wide', 'narrow')), may hold values from -0.109375 to 0.109375
- out_grad: bfloat16 [16, 1024, 768], P('wide', 'narrow'), may hold values from -6 to 6
Outputs:
- layer_out: bfloat16 [16, 1024, 768], P('wide', 'narrow')
- grad_in: bfloat16 [16, 1024, 768], P('wide', 'narrow')
- grad_in_proj: float32 [3, 768, 768], P(None, ('wide', 'narrow'))
- grad_out_proj: float32 [768, 768], P(('wide', 'narrow'))
- grad_vec_bias: float32 [6, 768], P(None, ('wide', 'narrow'))
- grad_norm_gain: float32 [2, 768], P(None, ('wide', 'narrow'))
- grad_ffn_in: float32 [768, 3072], P(('wide', 'narrow'))
- grad_ffn_bias: float32 [3072], P(('wide', 'narrow'))
- grad_ffn_out: float32 [3072, 768], P(('wide', 'narrow'))
The draws below stay inside these ranges and needn't reach their ends.
Inputs may be any that keep to these rules, and one draw needn't show every extreme that they name: `doc_ids`: documents are packed end to end in each slot. Along the positions of a slot the ids never fall; each of the 4 ids holds 1 to 512 consecutive positions, one of them exactly 512.
All inputs are finite; a program needn't handle non-finite values.
Results may differ from the reference program's by a relative error of at most 0.015.
Values may be sent and summed in bfloat16 or wider, within the bound.
No kernel may reach another device: no remote copies, remote signals or barrier semaphores. Data moves between devices by JAX's collectives and lax.ppermute only.
A program may use at most 192 MiB of HBM per device.

```python
import math
import jax
import jax.numpy as jnp
import numpy as np
from jax import lax

HEADS = 12
DH = 64
FF = 3072
D = 768
SHARD = 256
DOCS = 4
L = 1024
SLOTS = 16
N_NARROW = 4


def block_levels(key, shape, cuts, smallest, high):
    factor_of, own = 1.0, jax.random.fold_in(key, 6)
    for position, shards_of in cuts:
        heights = jnp.exp(jax.random.uniform(jax.random.fold_in(own, position), (shards_of,), jnp.float32, smallest / len(cuts), high / len(cuts)))
        factor_of = factor_of * jnp.repeat(heights, shape[position] // shards_of).reshape([-1 if axis == position else 1 for axis in range(len(shape))])
    return factor_of


def length_profile(number_of, total, limit, lean):
    weights = [(1 << 20) // math.isqrt(grade ** lean) + 1 for grade in range(2, number_of + 1)]
    rest, holding = total - limit - (number_of - 1), [1] * (number_of - 1)
    while rest > 0:
        candidates = [i for i in range(number_of - 1) if holding[i] < limit]
        mass, left = sum([weights[i] for i in candidates]), rest
        for i in candidates:
            extra = min(limit - holding[i], max(1, left * weights[i] // mass), rest)
            holding[i] = holding[i] + extra
            rest = rest - extra
    return np.array([limit] + holding)


def uneven_parts(stream_key, count, total, bound, lean):
    if count == 2:
        one = jax.random.randint(stream_key, (), max(1, total - bound), min(bound, total - 1) + 1)
        return jnp.stack([one, total - one])
    lengths = jnp.asarray(length_profile(count, total, bound, lean), jnp.int32)
    twos = (count - 1) // 2
    source_of, sink = lengths[1:1 + 2 * twos:2], lengths[2:2 + 2 * twos:2]
    slack = jnp.minimum(source_of - 1, bound - sink)
    moved = jax.random.randint(jax.random.fold_in(stream_key, 1), (twos,), 0, 1 << 20) % (slack + 1)
    lengths = lengths.at[1:1 + 2 * twos:2].set(source_of - moved).at[2:2 + 2 * twos:2].set(sink + moved)
    return lengths[jax.random.permutation(jax.random.fold_in(stream_key, 2), count)]


def noise(stream_key, extent, width, bound, pieces=(), held_as=jnp.bfloat16):
    values = width * jax.random.normal(stream_key, extent, jnp.float32)
    if pieces:
        values = values * block_levels(stream_key, extent, pieces, -0.22, 0.18)
    return jnp.clip(values, -bound, bound).astype(held_as)


def setup_inputs(seed: int = 0) -> dict:
    streams_of = jax.random.split(jax.random.key(seed), 11)
    return {
        "layer_in": noise(streams_of[0], (SLOTS, L, D), 1.0, 6.0, ((0, 8), (1, 4))),
        "doc_ids": jax.vmap(lambda own: jnp.searchsorted(jnp.cumsum(uneven_parts(own, DOCS, L, SHARD * N_NARROW // 2, 2)), jnp.arange(L), side="right"))(jax.random.split(streams_of[1], SLOTS)).reshape((SLOTS, L)).astype(jnp.int32),
        "in_proj": noise(streams_of[2], (3, D, D), D ** -0.5, 0.21875, ((1, 32),)),
        "out_proj": noise(streams_of[3], (D, D), (D // 64) ** -0.5, 1.75, ((0, 32),)),
        "vec_bias": noise(streams_of[4], (6, D), 0.3, 3.0, ((1, 32),)),
        "norm_gain": jnp.clip(1.0 + 0.1 * jax.random.normal(streams_of[5], (2, D), jnp.float32), 0.5, 1.5).astype(jnp.bfloat16),
        "ffn_in": noise(streams_of[6], (D, FF), D ** -0.5, 0.21875, ((0, 32),)),
        "ffn_bias": noise(streams_of[7], (FF,), 0.3, 3.0, ((0, 32),)),
        "ffn_out": noise(streams_of[8], (FF, D), FF ** -0.5, 0.109375, ((0, 32),)),
        "out_grad": noise(streams_of[9], (SLOTS, L, D), 1.0, 6.0, ((0, 8), (1, 4))),
    }


@jax.custom_vjp
def low(v):
    return lax.optimization_barrier(v.astype(jnp.bfloat16)).astype(jnp.float32)

@jax.custom_vjp
def low_back(v):
    return v

def low_keep(v):
    return (low(v), None)

def low_pass(kept, grad):
    return (grad,)

def back_keep(v):
    return (v, None)

def back_low(kept, grad):
    return (low(grad),)
low.defvjp(low_keep, low_pass)
low_back.defvjp(back_keep, back_low)
highest = lax.Precision.HIGHEST
eps = 1e-05

def product(left, right):
    return jnp.dot(left, right, precision=highest)

def layer_norm(rows_in, scale_vec, shift_vec):
    average = lax.optimization_barrier(jnp.mean(rows_in, -1, keepdims=True))
    centered = rows_in - average
    variance = lax.optimization_barrier(jnp.mean(centered * centered, -1, keepdims=True))
    return centered * lax.rsqrt(variance + eps) * scale_vec + shift_vec

def gelu_exact(upper):
    return 0.5 * upper * (1.0 + lax.erf(upper * 0.7071067811865476))

def attend_block(block_items):
    queries, key_heads, value_heads, ids_query, ids_key = block_items
    scores = low_back(jnp.einsum('qhd,khd->hqk', queries, key_heads, precision=highest))
    allowed = ids_query[:, None] == ids_key[None, :]
    scores = jnp.where(allowed[None], scores, -1000000000.0)
    row_top = lax.optimization_barrier(jnp.max(scores, -1, keepdims=True))
    exp_scores = jnp.exp(scores - row_top)
    attn_probs = exp_scores / lax.optimization_barrier(jnp.sum(exp_scores, -1, keepdims=True))
    probs_low = low(attn_probs)
    return jnp.einsum('hqk,khd->qhd', probs_low, value_heads, precision=highest)

def forward(weights, rows_in, ids_in):
    in_proj, out_proj, vec_bias, norm_gain, ffn_in, ffn_bias, ffn_out = weights
    group_size = rows_in.shape[0]
    tokens = rows_in.reshape(-1, D)
    queries = low(low_back((product(tokens, in_proj[0]) + vec_bias[0]) * 0.125))
    key_rows = low(low_back(product(tokens, in_proj[1])))
    value_rows = low(low_back(product(tokens, in_proj[2]) + vec_bias[1]))
    block = min(512, L)
    block_count = L // block
    query_blocks = queries.reshape(group_size * block_count, block, HEADS, DH)
    key_heads = jnp.repeat(key_rows.reshape(group_size, L, HEADS, DH), block_count, axis=0)
    value_heads = jnp.repeat(value_rows.reshape(group_size, L, HEADS, DH), block_count, axis=0)
    id_blocks = ids_in.reshape(group_size * block_count, block)
    id_keys = jnp.repeat(ids_in, block_count, axis=0)
    mixed_rows = lax.map(jax.checkpoint(attend_block), (query_blocks, key_heads, value_heads, id_blocks, id_keys))
    mixed_rows = low(low_back(mixed_rows.reshape(-1, D)))
    attn_out = low_back(product(mixed_rows, out_proj) + vec_bias[2])
    first_sum = tokens + attn_out
    normed = layer_norm(first_sum, norm_gain[0], vec_bias[3])
    upper = low_back(product(low(normed), ffn_in) + ffn_bias)
    active = low(gelu_exact(upper))
    down_out = low_back(product(active, ffn_out) + vec_bias[4])
    second_sum = normed + down_out
    return layer_norm(second_sum, norm_gain[1], vec_bias[5]).reshape(group_size, L, D)

def reference(layer_in, doc_ids, in_proj, out_proj, vec_bias, norm_gain, ffn_in, ffn_bias, ffn_out, out_grad):
    params = tuple([array_in.astype(jnp.float32) for array_in in (in_proj, out_proj, vec_bias, norm_gain, ffn_in, ffn_bias, ffn_out)])
    group_size = math.gcd(SLOTS, max(1, 4096 // L))
    group_count = SLOTS // group_size

    def regroup(array_in):
        return array_in.reshape((group_count, group_size) + array_in.shape[1:])

    def group_step(carry, group_items):
        rows_in, ids_in, grad_rows = group_items

        def run_layer(weights, inputs):
            return forward(weights, inputs, ids_in)
        result, pull = jax.vjp(run_layer, params, rows_in)
        grad_weights, grad_rows_in = pull(grad_rows)
        carry = jax.tree.map(jnp.add, carry, grad_weights)
        return (carry, (result.astype(jnp.bfloat16), grad_rows_in.astype(jnp.bfloat16)))
    zeros = tuple([jnp.zeros_like(param) for param in params])
    totals, outputs = lax.scan(group_step, zeros, (regroup(layer_in.astype(jnp.float32)), regroup(doc_ids), regroup(out_grad.astype(jnp.float32))))
    layer_out = outputs[0].reshape(SLOTS, L, D)
    grad_in = outputs[1].reshape(SLOTS, L, D)
    return (layer_out, grad_in, totals[0], totals[1], totals[2], totals[3], totals[4], totals[5], totals[6])
```

```python
import jax
import jax.numpy as jnp
from jax import lax
from jax.experimental import pallas as pl
from jax.experimental.pallas import tpu as pltpu
from jax.sharding import PartitionSpec as P

D = 768
FF = 3072
DH = 64
PAIR = 128
TRIO = 3 * PAIR
HALF = D // 2
QB = 256
AXES = ("wide", "narrow")
EPS = 1e-05
BF = jnp.bfloat16
F32 = jnp.float32
MASKED = -1000000000.0
SMALL = 128


def matmul(left, right):
    return jnp.dot(left, right, preferred_element_type=F32)


def times_transposed(left, right):
    return lax.dot_general(left, right, (((1,), (1,)), ((), ())), preferred_element_type=F32)


def left_inner(left, right):
    return lax.dot_general(left, right, (((0,), (0,)), ((), ())), preferred_element_type=F32)


def attend_kernel(trio_ref, id_col_ref, id_row_ref, mixed_ref, lse_ref):
    total = trio_ref.shape[0]

    def block(step, carry):
        rows = pl.ds(pl.multiple_of(step * QB, QB), QB)
        same = id_col_ref[...] == id_row_ref[:, rows]
        pieces = []
        for head in range(2):
            q = trio_ref[rows, head * DH : (head + 1) * DH]
            k = trio_ref[:, PAIR + head * DH : PAIR + (head + 1) * DH]
            v = trio_ref[:, 2 * PAIR + head * DH : 2 * PAIR + (head + 1) * DH]
            scores = jnp.where(same, times_transposed(k, q), MASKED)
            top = jnp.max(scores, 0, keepdims=True)
            weights = jnp.exp(scores - top)
            mass = jnp.sum(weights, 0, keepdims=True)
            pieces.append(left_inner(v, weights.astype(BF)) / mass)
            lse_ref[0, head : head + 1, rows] = top + jnp.log(mass)
        mixed_ref[rows, :] = jnp.concatenate(pieces, 0).T.astype(BF)
        return carry

    lax.fori_loop(0, total // QB, block, 0)


def attend(trios, id_col, id_row):
    total, width = trios.shape
    pairs = width // TRIO
    return pl.pallas_call(
        attend_kernel,
        grid=(pairs,),
        in_specs=[
            pl.BlockSpec((total, TRIO), lambda p: (0, p)),
            pl.BlockSpec((total, 1), lambda p: (0, 0)),
            pl.BlockSpec((1, total), lambda p: (0, 0)),
        ],
        out_specs=[
            pl.BlockSpec((total, PAIR), lambda p: (0, p)),
            pl.BlockSpec((1, 2, total), lambda p: (p, 0, 0)),
        ],
        out_shape=[
            jax.ShapeDtypeStruct((total, pairs * PAIR), BF),
            jax.ShapeDtypeStruct((pairs, 2, total), F32),
        ],
        cost_estimate=pl.CostEstimate(
            flops=4 * total * total * PAIR * pairs * 4,
            transcendentals=2 * pairs * total * total,
            bytes_accessed=total * width * 4,
        ),
        name="attend",
    )(trios, id_col, id_row)


def attend_back_kernel(trio_ref, grad_ref, id_col_ref, id_row_ref, lse_ref, out_ref, dk_ref, dv_ref):
    total = trio_ref.shape[0]
    dk_ref[...] = jnp.zeros_like(dk_ref)
    dv_ref[...] = jnp.zeros_like(dv_ref)

    def block(step, carry):
        rows = pl.ds(pl.multiple_of(step * QB, QB), QB)
        same = id_col_ref[...] == id_row_ref[:, rows]
        pieces = []
        for head in range(2):
            lanes = slice(head * DH, (head + 1) * DH)
            q = trio_ref[rows, lanes]
            k = trio_ref[:, PAIR + head * DH : PAIR + (head + 1) * DH]
            v = trio_ref[:, 2 * PAIR + head * DH : 2 * PAIR + (head + 1) * DH]
            g = grad_ref[rows, lanes]
            scores = times_transposed(k, q) - lse_ref[0, head : head + 1, rows]
            probs = jnp.where(same, jnp.exp(scores), 0.0)
            grad_probs = times_transposed(v, g)
            inner = jnp.sum(probs * grad_probs, 0, keepdims=True)
            grad_scores = (probs * (grad_probs - inner)).astype(BF)
            pieces.append(left_inner(k, grad_scores))
            dk_ref[:, lanes] += matmul(grad_scores, q)
            dv_ref[:, lanes] += matmul(probs.astype(BF), g)
        grad_q = jnp.concatenate(pieces, 0).T.astype(BF)
        out_ref[rows, :PAIR] = (grad_q.astype(F32) * 0.125).astype(BF)
        return carry

    lax.fori_loop(0, total // QB, block, 0)
    out_ref[:, PAIR : 2 * PAIR] = dk_ref[...].astype(BF)
    out_ref[:, 2 * PAIR :] = dv_ref[...].astype(BF)


def attend_back(trios, grads, id_col, id_row, lse):
    total, width = trios.shape
    pairs = width // TRIO
    return pl.pallas_call(
        attend_back_kernel,
        grid=(pairs,),
        in_specs=[
            pl.BlockSpec((total, TRIO), lambda p: (0, p)),
            pl.BlockSpec((total, PAIR), lambda p: (0, p)),
            pl.BlockSpec((total, 1), lambda p: (0, 0)),
            pl.BlockSpec((1, total), lambda p: (0, 0)),
            pl.BlockSpec((1, 2, total), lambda p: (p, 0, 0)),
        ],
        out_specs=pl.BlockSpec((total, TRIO), lambda p: (0, p)),
        out_shape=jax.ShapeDtypeStruct((total, width), BF),
        scratch_shapes=[pltpu.VMEM((total, PAIR), F32), pltpu.VMEM((total, PAIR), F32)],
        cost_estimate=pl.CostEstimate(
            flops=10 * total * total * PAIR * pairs * 4,
            transcendentals=2 * pairs * total * total,
            bytes_accessed=total * width * 6,
        ),
        name="attend_back",
    )(trios, grads, id_col, id_row, lse)


class Links:
    def __init__(self, mesh):
        self.devices = mesh.shape["wide"] * mesh.shape["narrow"]
        self.chips = self.devices // 2
        bits = self.chips.bit_length() - 1
        assert self.chips == 1 << bits
        self.groups = [(low, 2) for low in range(bits - 2, -1, -2)]
        if bits % 2:
            self.groups.append((0, 1))
        self.own = lax.axis_index(AXES)
        self.chip = self.own // 2
        self.core = self.own % 2

    def send(self, value, flip_even, flip_odd):
        pairs = [(d, d ^ (flip_odd if d % 2 else flip_even)) for d in range(self.devices)]
        return lax.ppermute(value, AXES, pairs)

    def core_swap(self, value):
        return self.send(value, 1, 1)

    def row_swap(self, value):
        return self.send(value, 2, 2)

    def gather(self, block):
        have = block[None]
        for low, size in self.groups:
            place = (self.chip >> low) % (1 << size)
            width = 1 << size
            full = jnp.zeros((have.shape[0], width) + block.shape, block.dtype)

            def put(full, piece, at):
                return lax.dynamic_update_slice_in_dim(full, piece[:, None], at, 1)

            full = put(full, have, place)
            if size == 1:
                full = put(full, self.send(have, 2 << low, 2 << low), place ^ 1)
            else:
                first, second = 1 + self.core, 2 - self.core
                one = self.send(have, 2 << low, 4 << low)
                two = self.send(jnp.stack([have, one]), 4 << low, 2 << low)
                full = put(full, one, place ^ first)
                full = put(full, two[0], place ^ second)
                full = put(full, two[1], place ^ 3)
            have = full.reshape((-1,) + block.shape)
        return have

    def scatter_sum(self, blocks):
        have = blocks
        for low, size in reversed(self.groups):
            place = (self.chip >> low) % (1 << size)
            width = 1 << size
            parts = have.reshape((-1, width) + blocks.shape[1:])

            def take(at):
                return lax.dynamic_index_in_dim(parts, at, 1, keepdims=False)

            if size == 1:
                got = self.send(take(place ^ 1).astype(BF), 2 << low, 2 << low)
                have = take(place).astype(F32) + got.astype(F32)
            else:
                first, second = 1 + self.core, 2 - self.core
                two = jnp.stack([take(place ^ second), take(place ^ 3)]).astype(BF)
                two = self.send(two, 4 << low, 2 << low)
                one = take(place ^ first).astype(F32) + two[1].astype(F32)
                one = self.send(one.astype(BF), 2 << low, 4 << low)
                have = take(place).astype(F32) + two[0].astype(F32) + one.astype(F32)
        return have[0] if have.ndim == blocks.ndim else have


def pick(parts, at, axis):
    return lax.dynamic_index_in_dim(parts, at, axis, keepdims=False)


def by_core(core, own, other, axis):
    return jnp.where(
        core == 0, jnp.concatenate([own, other], axis), jnp.concatenate([other, own], axis)
    )


def normalize(rows):
    average = jnp.mean(rows, -1, keepdims=True)
    centered = rows - average
    scale = lax.rsqrt(jnp.mean(centered * centered, -1, keepdims=True) + EPS)
    return centered * scale, scale


def normalize_back(grads, normal, scale):
    return (
        grads
        - jnp.mean(grads, -1, keepdims=True)
        - normal * jnp.mean(grads * normal, -1, keepdims=True)
    ) * scale


def local(mesh):
    def run(
        layer_in, doc_ids, in_proj, out_proj, vec_bias, norm_gain, ffn_in, ffn_bias, ffn_out, out_grad
    ):
        links = Links(mesh)
        core, chips = links.core, links.chips
        side = (links.own // 2) % 2
        slots, shard, _ = layer_in.shape
        assert slots == 2 and mesh.shape["narrow"] == 4
        own_rows = in_proj.shape[1]
        chip_rows = 2 * own_rows
        hidden = ffn_out.shape[0]

        trio_cols = in_proj.reshape(3, own_rows, 2, 3, PAIR).transpose(1, 2, 3, 0, 4)
        trio_cols = trio_cols.reshape(own_rows, 2, 3 * TRIO)
        ffn_cols = ffn_in.reshape(own_rows, chips, 2, hidden).transpose(0, 2, 1, 3)
        ffn_cols = ffn_cols.reshape(own_rows, 2, chips * hidden)
        vectors = jnp.concatenate([vec_bias, norm_gain], 0).T
        vectors = jnp.pad(vectors, ((0, 0), (0, SMALL - 8)))
        cols = jnp.concatenate([trio_cols, ffn_cols], 2)
        mine = jnp.concatenate([pick(cols, core, 1), vectors], 1)
        other = jnp.concatenate([pick(cols, 1 - core, 1), vectors], 1)
        cols = by_core(core, mine, links.core_swap(other), 0)
        split = 3 * TRIO
        out_part = out_proj.reshape(own_rows, 2, HALF).transpose(1, 0, 2).reshape(chip_rows, HALF)
        small = jnp.concatenate(
            [
                cols[:, split + FF // 2 :][:, :8],
                ffn_bias.reshape(chip_rows, 2),
                jnp.zeros((chip_rows, SMALL - 10), BF),
            ],
            1,
        )

        keep = pick(layer_in, side, 0)
        tokens = jnp.concatenate([keep, links.row_swap(pick(layer_in, 1 - side, 0))], 0)
        attn_pack = links.gather(jnp.concatenate([cols[:, :split], out_part, small], 1))
        all_tokens = jnp.concatenate([tokens, links.core_swap(tokens)], 0)
        down_weight = links.gather(ffn_out).reshape(chips * hidden, D)
        up_weight = links.gather(cols[:, split : split + FF // 2]).reshape(D, FF // 2)
        keep = pick(out_grad, side, 0)
        grad_out = jnp.concatenate([keep, links.row_swap(pick(out_grad, 1 - side, 0))], 0)
        grad_out = grad_out.astype(F32)

        trio_weight = attn_pack[..., :split].reshape(D, split)
        out_own = attn_pack[..., split : split + HALF].reshape(chips, 2, own_rows, HALF)
        out_own = out_own.transpose(0, 2, 1, 3).reshape(chips, 1, own_rows, D)
        out_weight = by_core(core, out_own, links.core_swap(out_own), 1).reshape(D, D)
        small = attn_pack[..., split + HALF :]
        bias = small[..., :8].reshape(D, 8).T.astype(F32)
        up_bias = small[..., 8:10].reshape(FF // 2).astype(F32)

        slot_ids = pick(doc_ids, side, 0).reshape(2, 2, shard)
        slot_ids = jnp.stack(
            [
                slot_ids[side, core],
                slot_ids[1 - side, core],
                slot_ids[side, 1 - core],
                slot_ids[1 - side, 1 - core],
            ]
        )
        id_col = slot_ids.reshape(-1, 1)
        id_row = slot_ids.reshape(1, -1)

        own_bias = pick(bias[:2].reshape(2, 2, 3, PAIR), core, 1)
        zero = jnp.zeros_like(own_bias[0])
        trio_bias = jnp.stack([own_bias[0], zero, own_bias[1]], 1).reshape(1, split)
        trio_scale = jnp.concatenate([zero + 0.125, zero + 1.0, zero + 1.0], 1).reshape(1, split)
        trios = ((matmul(all_tokens, trio_weight) + trio_bias) * trio_scale).astype(BF)
        mixed_heads, lse = attend(trios, id_col, id_row)
        count = tokens.shape[0]
        mixed = by_core(core, mixed_heads[:count], links.core_swap(mixed_heads[count:]), 1)

        first_sum = tokens.astype(F32) + matmul(mixed, out_weight) + bias[2]
        first_normal, first_scale = normalize(first_sum)
        normed = first_normal * bias[6] + bias[3]
        normed_low = normed.astype(BF)
        all_normed = jnp.concatenate([normed_low, links.core_swap(normed_low)], 0)
        upper = matmul(all_normed, up_weight) + up_bias
        erf_part = 1.0 + lax.erf(upper * 0.7071067811865476)
        active = (0.5 * upper * erf_part).astype(BF)
        partial = matmul(active, down_weight)
        second_sum = (
            normed
            + partial[:count]
            + links.core_swap(partial[count:].astype(BF)).astype(F32)
            + bias[4]
        )
        second_normal, second_scale = normalize(second_sum)
        result = (second_normal * bias[7] + bias[5]).astype(BF)

        def home(rows):
            got = links.row_swap(rows[shard:])
            kept = rows[:shard]
            return jnp.where(side == 0, jnp.stack([kept, got]), jnp.stack([got, kept]))

        layer_out = home(result)

        grad_second = normalize_back(grad_out * bias[7], second_normal, second_scale)
        grad_down = grad_second.astype(BF)
        all_down = jnp.concatenate([grad_down, links.core_swap(grad_down)], 0)
        grad_down_weight = left_inner(active, all_down).astype(BF)
        grad_active = times_transposed(all_down, down_weight)
        slope = 0.5 * erf_part + upper * jnp.exp(-0.5 * upper * upper) * 0.3989422804014327
        grad_upper = (grad_active * slope).astype(BF)
        grad_up_weight = left_inner(all_normed, grad_upper).astype(BF)
        partial = times_transposed(grad_upper, up_weight)
        grad_normed = (
            grad_second
            + partial[:count]
            + links.core_swap(partial[count:].astype(BF)).astype(F32)
        )
        grad_first = normalize_back(grad_normed * bias[6], first_normal, first_scale)
        grad_attn = grad_first.astype(BF)
        grad_out_weight = left_inner(mixed, grad_attn).reshape(chips, 2, own_rows, D)
        grad_mixed = times_transposed(grad_attn, out_weight).astype(BF).reshape(count, 2, HALF)
        grad_heads = jnp.concatenate(
            [pick(grad_mixed, core, 1), links.core_swap(pick(grad_mixed, 1 - core, 1))], 0
        )
        grad_trios = attend_back(trios, grad_heads, id_col, id_row, lse)
        grad_trio_weight = left_inner(all_tokens, grad_trios).astype(BF)
        partial = times_transposed(grad_trios, trio_weight)
        grad_tokens = (
            grad_first
            + partial[:count]
            + links.core_swap(partial[count:].astype(BF)).astype(F32)
        )
        grad_in = home(grad_tokens.astype(BF))

        down_total = links.scatter_sum(grad_down_weight.reshape(chips, hidden, D))
        up_total = links.scatter_sum(grad_up_weight.reshape(chips, chip_rows, FF // 2))
        sent = links.core_swap(pick(grad_out_weight, 1 - core, 1).astype(BF))
        out_sum = pick(grad_out_weight, core, 1) + sent.astype(F32)
        out_sum = out_sum.astype(BF).reshape(chips, own_rows, 2, HALF).transpose(0, 2, 1, 3)
        out_sum = out_sum.reshape(chips, chip_rows, HALF)
        trio_sums = jnp.sum(grad_trios.astype(F32), 0).reshape(3, 3, PAIR)
        own_half = jnp.stack([trio_sums[:, 0].reshape(HALF), trio_sums[:, 2].reshape(HALF)])
        none = jnp.zeros_like(own_half)
        sums = jnp.concatenate(
            [
                by_core(core, own_half, none, 1),
                jnp.stack(
                    [
                        jnp.sum(grad_attn.astype(F32), 0),
                        jnp.sum(grad_normed, 0),
                        jnp.sum(grad_down.astype(F32), 0),
                        jnp.sum(grad_out, 0),
                        jnp.sum(grad_normed * first_normal, 0),
                        jnp.sum(grad_out * second_normal, 0),
                    ]
                ),
            ],
            0,
        )
        up_bias_sum = jnp.sum(grad_upper.astype(F32), 0).reshape(chips, chip_rows, 2)
        small = jnp.concatenate(
            [
                sums.T.reshape(chips, chip_rows, 8),
                up_bias_sum,
                jnp.zeros((chips, chip_rows, SMALL - 10), F32),
            ],
            2,
        ).astype(BF)
        attn_total = links.scatter_sum(
            jnp.concatenate(
                [grad_trio_weight.reshape(chips, chip_rows, split), out_sum, small], 2
            )
        )

        up_rows = up_total.reshape(2, own_rows, FF // 2)
        attn_rows = attn_total.reshape(2, own_rows, -1)
        packed = jnp.concatenate([attn_rows[..., :split], attn_rows[..., split + HALF :]], 2)
        mine, other = pick(packed, core, 0), pick(packed, 1 - core, 0)
        got = links.core_swap(other.astype(BF)).astype(F32)
        grad_in_proj = by_core(
            core,
            mine[:, :split].reshape(own_rows, 1, 3, 3, PAIR),
            got[:, :split].reshape(own_rows, 1, 3, 3, PAIR),
            1,
        )
        grad_in_proj = grad_in_proj.transpose(3, 0, 1, 2, 4).reshape(3, own_rows, D)
        grad_out_proj = attn_total[:, split : split + HALF].reshape(2, own_rows, HALF)
        grad_out_proj = grad_out_proj.transpose(1, 0, 2).reshape(own_rows, D)
        vectors = (mine[:, split : split + 8] + got[:, split : split + 8]).T
        grad_ffn_bias = attn_total[:, split + HALF + 8 : split + HALF + 10].reshape(hidden)
        got = links.core_swap(pick(up_rows, 1 - core, 0).astype(BF)).astype(F32)
        grad_ffn_in = by_core(
            core,
            pick(up_rows, core, 0).reshape(own_rows, chips, 1, hidden),
            got.reshape(own_rows, chips, 1, hidden),
            2,
        ).reshape(own_rows, FF)
        return (
            layer_out,
            grad_in,
            grad_in_proj,
            grad_out_proj,
            vectors[:6],
            vectors[6:],
            grad_ffn_in,
            grad_ffn_bias,
            down_total,
        )

    return run


def solution(mesh):
    return jax.shard_map(
        local(mesh),
        mesh=mesh,
        in_specs=(
            P("wide", "narrow", None),
            P("wide", None),
            P(None, AXES, None),
            P(AXES, None),
            P(None, AXES),
            P(None, AXES),
            P(AXES, None),
            P(AXES),
            P(AXES, None),
            P("wide", "narrow", None),
        ),
        out_specs=(
            P("wide", "narrow", None),
            P("wide", "narrow", None),
            P(None, AXES, None),
            P(AXES, None),
            P(None, AXES),
            P(None, AXES),
            P(AXES, None),
            P(AXES),
            P(AXES, None),
        ),
        check_vma=False,
    )
```

```python
import functools

import jax
import jax.numpy as jnp
from jax import lax
from jax.experimental import pallas as pl
from jax.experimental.pallas import tpu as pltpu
from jax.sharding import PartitionSpec as P

D = 768
FF = 3072
DH = 64
PAIR = 128
HALF = D // 2
QB = 256
AXES = ("wide", "narrow")
EPS = 1e-05
BF = jnp.bfloat16
F32 = jnp.float32
MASKED = -1000000000.0
SMALL = 128
BRIEF = pl.CostEstimate(flops=1000, transcendentals=0, bytes_accessed=1000)


def matmul(left, right):
    return jnp.dot(left, right, preferred_element_type=F32)


def times_transposed(left, right):
    return lax.dot_general(left, right, (((1,), (1,)), ((), ())), preferred_element_type=F32)


def left_inner(left, right):
    return lax.dot_general(left, right, (((0,), (0,)), ((), ())), preferred_element_type=F32)


def overlap(low_ref, high_ref, key_block, query_block):
    return (low_ref[key_block] <= high_ref[query_block]) & (
        low_ref[query_block] <= high_ref[key_block]
    )


def tile_ids(id_col_ref, id_row_ref, keys, queries):
    return id_col_ref[keys, :] == id_row_ref[:, queries]


def one_head(rows, head):
    lane = lax.broadcasted_iota(jnp.int32, rows.shape, 1)
    return jnp.where((lane < DH) if head % 2 == 0 else (lane >= DH), rows, jnp.zeros_like(rows))


def attend_kernel(
    low_ref, high_ref, trio_ref, id_col_ref, id_row_ref, mixed_ref, lse_ref, vt_ref, acc_ref, top_ref, mass_ref
):
    total = trio_ref.shape[0]
    heads = HALF // DH
    blocks = total // QB
    vt_ref[...] = trio_ref[:, 2 * HALF :].T
    acc_ref[...] = jnp.zeros_like(acc_ref)
    mass_ref[...] = jnp.zeros_like(mass_ref)
    top_ref[...] = jnp.full_like(top_ref, -jnp.inf)

    def tile(step, carry):
        query_block, key_block = step // blocks, step % blocks

        @pl.when(overlap(low_ref, high_ref, key_block, query_block))
        def _():
            queries = pl.ds(pl.multiple_of(query_block * QB, QB), QB)
            keys = pl.ds(pl.multiple_of(key_block * QB, QB), QB)
            same = tile_ids(id_col_ref, id_row_ref, keys, queries)
            old_tops = top_ref[:, queries]
            old_mass = mass_ref[:, queries]

            def score(head):
                lanes = slice(head // 2 * PAIR, head // 2 * PAIR + PAIR)
                q = one_head(trio_ref[queries, lanes], head)
                k = trio_ref[keys, HALF + lanes.start : HALF + lanes.stop]
                return jnp.where(same, times_transposed(k, q), MASKED)

            scores = [score(head) for head in range(heads)]
            tops = [jnp.maximum(old_tops[h : h + 1], jnp.max(scores[h], 0, keepdims=True)) for h in range(heads)]
            weights = [jnp.exp(scores[h] - tops[h]) for h in range(heads)]
            shrinks = [jnp.exp(old_tops[h : h + 1] - tops[h]) for h in range(heads)]
            masses = [old_mass[h : h + 1] * shrinks[h] + jnp.sum(weights[h], 0, keepdims=True) for h in range(heads)]
            outs = [matmul(vt_ref[h * DH : (h + 1) * DH, keys], weights[h].astype(BF)) for h in range(heads)]
            for h in range(heads):
                rows = slice(h * DH, (h + 1) * DH)
                acc_ref[rows, queries] = acc_ref[rows, queries] * shrinks[h] + outs[h]
            top_ref[:, queries] = jnp.concatenate(tops + [old_tops[heads:]], 0)
            mass_ref[:, queries] = jnp.concatenate(masses + [old_mass[heads:]], 0)

        return carry

    lax.fori_loop(0, blocks * blocks, tile, 0)
    for head in range(heads):
        rows = slice(head * DH, (head + 1) * DH)
        acc_ref[rows, :] = acc_ref[rows, :] / mass_ref[head : head + 1, :]
    mixed_ref[...] = acc_ref[...].T.astype(BF)
    lse_ref[...] = top_ref[...] + jnp.log(mass_ref[...])


def attend(trios, low, high, id_col, id_row):
    total, width = trios.shape
    return pl.pallas_call(
        attend_kernel,
        grid_spec=pltpu.PrefetchScalarGridSpec(
            num_scalar_prefetch=2,
            grid=(1,),
            in_specs=[
                pl.BlockSpec((total, width), lambda p, *_: (0, 0)),
                pl.BlockSpec((total, 1), lambda p, *_: (0, 0)),
                pl.BlockSpec((1, total), lambda p, *_: (0, 0)),
            ],
            out_specs=[
                pl.BlockSpec((total, HALF), lambda p, *_: (0, 0)),
                pl.BlockSpec((8, total), lambda p, *_: (0, 0)),
            ],
            scratch_shapes=[
                pltpu.VMEM((HALF, total), BF),
                pltpu.VMEM((HALF, total), F32),
                pltpu.VMEM((8, total), F32),
                pltpu.VMEM((8, total), F32),
            ],
        ),
        out_shape=[
            jax.ShapeDtypeStruct((total, HALF), BF),
            jax.ShapeDtypeStruct((8, total), F32),
        ],
        cost_estimate=BRIEF,
        name="attend",
    )(low, high, trios, id_col, id_row)


def attend_back_kernel(
    low_ref,
    high_ref,
    trio_ref,
    grad_ref,
    mixed_ref,
    id_col_ref,
    id_row_ref,
    lse_ref,
    out_ref,
    kt_ref,
    inner_ref,
    dq_ref,
    dk_ref,
    dv_ref,
):
    total = trio_ref.shape[0]
    heads = HALF // DH
    blocks = total // QB
    kt_ref[...] = trio_ref[:, HALF : 2 * HALF].T
    dq_ref[...] = jnp.zeros_like(dq_ref)
    dk_ref[...] = jnp.zeros_like(dk_ref)
    dv_ref[...] = jnp.zeros_like(dv_ref)
    lane = lax.broadcasted_iota(jnp.int32, (8, HALF), 1)
    row = lax.broadcasted_iota(jnp.int32, (8, HALF), 0)
    chosen = jnp.where(lane // DH == row, 1.0, 0.0)
    products = grad_ref[...].astype(F32) * mixed_ref[...].astype(F32)
    inner_ref[...] = lax.dot_general(
        chosen,
        products,
        (((1,), (1,)), ((), ())),
        precision=lax.Precision.HIGHEST,
        preferred_element_type=F32,
    )

    def tile(step, carry):
        query_block, key_block = step // blocks, step % blocks

        @pl.when(overlap(low_ref, high_ref, key_block, query_block))
        def _():
            queries = pl.ds(pl.multiple_of(query_block * QB, QB), QB)
            keys = pl.ds(pl.multiple_of(key_block * QB, QB), QB)
            same = tile_ids(id_col_ref, id_row_ref, keys, queries)
            tops = lse_ref[:, queries]
            inner = inner_ref[:, queries]
            q, k, v, g = [], [], [], []
            for head in range(heads):
                lanes = slice(head // 2 * PAIR, head // 2 * PAIR + PAIR)
                q.append(one_head(trio_ref[queries, lanes], head))
                g.append(one_head(grad_ref[queries, lanes], head))
                k.append(trio_ref[keys, HALF + lanes.start : HALF + lanes.stop])
                v.append(trio_ref[keys, 2 * HALF + lanes.start : 2 * HALF + lanes.stop])
            scores = [times_transposed(k[h], q[h]) for h in range(heads)]
            grad_probs = [times_transposed(v[h], g[h]) for h in range(heads)]
            probs = [jnp.where(same, jnp.exp(scores[h] - tops[h : h + 1]), 0.0) for h in range(heads)]
            grad_scores = [(probs[h] * (grad_probs[h] - inner[h : h + 1])).astype(BF) for h in range(heads)]
            probs = [probs[h].astype(BF) for h in range(heads)]
            dq = [matmul(kt_ref[h * DH : (h + 1) * DH, keys], grad_scores[h]) for h in range(heads)]
            dk = [matmul(grad_scores[h], q[h]) for h in range(heads)]
            dv = [matmul(probs[h], g[h]) for h in range(heads)]
            for h in range(heads):
                dq_ref[h * DH : (h + 1) * DH, queries] += dq[h]
            for pair in range(heads // 2):
                lanes = slice(pair * PAIR, pair * PAIR + PAIR)
                dk_ref[keys, lanes] += dk[2 * pair] + dk[2 * pair + 1]
                dv_ref[keys, lanes] += dv[2 * pair] + dv[2 * pair + 1]

        return carry

    lax.fori_loop(0, blocks * blocks, tile, 0)
    out_ref[:, :HALF] = (dq_ref[...].T.astype(BF).astype(F32) * 0.125).astype(BF)
    out_ref[:, HALF : 2 * HALF] = dk_ref[...].astype(BF)
    out_ref[:, 2 * HALF :] = dv_ref[...].astype(BF)


def attend_back(trios, grads, mixed, low, high, id_col, id_row, lse):
    total, width = trios.shape
    return pl.pallas_call(
        attend_back_kernel,
        grid_spec=pltpu.PrefetchScalarGridSpec(
            num_scalar_prefetch=2,
            grid=(1,),
            in_specs=[
                pl.BlockSpec((total, width), lambda p, *_: (0, 0)),
                pl.BlockSpec((total, HALF), lambda p, *_: (0, 0)),
                pl.BlockSpec((total, HALF), lambda p, *_: (0, 0)),
                pl.BlockSpec((total, 1), lambda p, *_: (0, 0)),
                pl.BlockSpec((1, total), lambda p, *_: (0, 0)),
                pl.BlockSpec((8, total), lambda p, *_: (0, 0)),
            ],
            out_specs=pl.BlockSpec((total, width), lambda p, *_: (0, 0)),
            scratch_shapes=[
                pltpu.VMEM((HALF, total), BF),
                pltpu.VMEM((8, total), F32),
                pltpu.VMEM((HALF, total), F32),
                pltpu.VMEM((total, HALF), F32),
                pltpu.VMEM((total, HALF), F32),
            ],
        ),
        out_shape=jax.ShapeDtypeStruct((total, width), BF),
        cost_estimate=BRIEF,
        name="attend_back",
    )(low, high, trios, grads, mixed, id_col, id_row, lse)


def place_kernel(columns, index_ref, *refs):
    count = (len(refs) - 2 - len(columns)) // 2
    pieces, outs = refs[:count], refs[count : count + len(columns)]
    held = refs[count + len(columns) : -2]
    in_sem, out_sem = refs[-2:]
    arriving = [
        pltpu.make_async_copy(pieces[i], held[i], in_sem.at[i]) for i in range(count)
    ]
    for copy in arriving:
        copy.start()
    leaving = []
    for i in range(count):
        arriving[i].wait()
        for j, (start, stop) in enumerate(columns):
            copy = pltpu.make_async_copy(
                held[i].at[:, :, start:stop], outs[j].at[:, index_ref[i]], out_sem.at[i, j]
            )
            copy.start()
            leaving.append(copy)
    for copy in leaving:
        copy.wait()


def place(pieces, index, columns):
    count = len(pieces)
    outer, rows, _ = pieces[0].shape
    anywhere = pl.BlockSpec(memory_space=pl.ANY)
    return pl.pallas_call(
        functools.partial(place_kernel, columns),
        grid_spec=pltpu.PrefetchScalarGridSpec(
            num_scalar_prefetch=1,
            grid=(1,),
            in_specs=[anywhere] * count,
            out_specs=[anywhere] * len(columns),
            scratch_shapes=[pltpu.VMEM(piece.shape, piece.dtype) for piece in pieces]
            + [pltpu.SemaphoreType.DMA((count,)), pltpu.SemaphoreType.DMA((count, len(columns)))],
        ),
        out_shape=[
            jax.ShapeDtypeStruct((outer, count, rows, stop - start), pieces[0].dtype)
            for start, stop in columns
        ],
        cost_estimate=BRIEF,
        name="place",
    )(index, *pieces)


def take_kernel(columns, count, index_ref, *refs):
    arrays = refs[: len(columns)]
    outs = refs[len(columns) : len(columns) + count]
    held = refs[len(columns) + count : -2]
    in_sem, out_sem = refs[-2:]
    arriving = []
    for i in range(count):
        for j, (start, stop) in enumerate(columns):
            copy = pltpu.make_async_copy(
                arrays[j].at[:, index_ref[i]], held[i].at[:, :, start:stop], in_sem.at[i, j]
            )
            copy.start()
            arriving.append(copy)
    leaving = []
    for i in range(count):
        for copy in arriving[i * len(columns) : (i + 1) * len(columns)]:
            copy.wait()
        copy = pltpu.make_async_copy(held[i], outs[i], out_sem.at[i])
        copy.start()
        leaving.append(copy)
    for copy in leaving:
        copy.wait()


def take(arrays, index):
    outer, count, rows, _ = arrays[0].shape
    columns, start = [], 0
    for array in arrays:
        columns.append((start, start + array.shape[3]))
        start += array.shape[3]
    anywhere = pl.BlockSpec(memory_space=pl.ANY)
    return pl.pallas_call(
        functools.partial(take_kernel, tuple(columns), count),
        grid_spec=pltpu.PrefetchScalarGridSpec(
            num_scalar_prefetch=1,
            grid=(1,),
            in_specs=[anywhere] * len(arrays),
            out_specs=[anywhere] * count,
            scratch_shapes=[pltpu.VMEM((outer, rows, start), BF) for _ in range(count)]
            + [pltpu.SemaphoreType.DMA((count, len(arrays))), pltpu.SemaphoreType.DMA((count,))],
        ),
        out_shape=[jax.ShapeDtypeStruct((outer, rows, start), BF)] * count,
        cost_estimate=BRIEF,
        name="take",
    )(index, *arrays)


class Links:
    def __init__(self, mesh):
        self.devices = mesh.shape["wide"] * mesh.shape["narrow"]
        self.chips = self.devices // 2
        bits = self.chips.bit_length() - 1
        assert self.chips == 1 << bits
        self.groups = [(low, 2) for low in range(bits - 2, -1, -2)]
        if bits % 2:
            self.groups.append((0, 1))
        self.own = lax.axis_index(AXES)
        self.chip = self.own // 2
        self.core = self.own % 2

    def send(self, value, flip_even, flip_odd):
        pairs = [(d, d ^ (flip_odd if d % 2 else flip_even)) for d in range(self.devices)]
        return lax.ppermute(value, AXES, pairs)

    def core_swap(self, value):
        return self.send(value, 1, 1)

    def row_swap(self, value):
        return self.send(value, 2, 2)

    def spots(self, low, size):
        place = (self.chip >> low) % (1 << size)
        if size == 1:
            return jnp.stack([place, place ^ 1]).astype(jnp.int32)
        first, second = 1 + self.core, 2 - self.core
        return jnp.stack([place, place ^ first, place ^ second, place ^ 3]).astype(jnp.int32)

    def gather(self, block, high, columns=None):
        width = block.shape[1]
        have = block[None]
        groups = self.groups if high else self.groups[::-1]
        for stage, (low, size) in enumerate(groups):
            if size == 1:
                (one,) = yield (self.send(have, 2 << low, 2 << low),)
                yield ()
                pieces = [have, one]
            else:
                one = self.send(have, 2 << low, 4 << low)
                two = self.send(have, 4 << low, 2 << low)
                one, two = yield (one, two)
                (three,) = yield (self.send(one, 4 << low, 2 << low),)
                pieces = [have, one, two, three]
            last = stage == len(groups) - 1
            placed = place(pieces, self.spots(low, size), columns if last and columns else ((0, width),))
            if high:
                placed = [out.reshape((-1,) + out.shape[2:]) for out in placed]
            else:
                placed = [out.reshape(1, -1, out.shape[3]) for out in placed]
            placed = yield tuple(placed)
            have = placed[0]

    def scatter(self, arrays, high):
        groups = self.groups if high else self.groups[::-1]
        for low, size in groups:
            if high:
                parts = [a.reshape((1, 1 << size, -1) + a.shape[2:]) for a in arrays]
            else:
                parts = [a.reshape((-1, 1 << size) + a.shape[1:]) for a in arrays]
            pieces = yield tuple(take(parts, self.spots(low, size)))
            if size == 1:
                (got,) = yield (self.send(pieces[1], 2 << low, 2 << low),)
                yield ()
                have = pieces[0].astype(F32) + got.astype(F32)
            else:
                three = self.send(pieces[3], 4 << low, 2 << low)
                two = self.send(pieces[2], 4 << low, 2 << low)
                three, two = yield (three, two)
                one = (pieces[1].astype(F32) + three.astype(F32)).astype(BF)
                (one,) = yield (self.send(one, 2 << low, 4 << low),)
                have = pieces[0].astype(F32) + two.astype(F32) + one.astype(F32)
            arrays = [have.astype(BF)]
        yield (have[0],)


class Flow:
    def __init__(self, steps):
        self.steps = steps
        self.pending = next(steps)
        self.running = True

    def go(self, values):
        try:
            self.pending = self.steps.send(values)
        except StopIteration:
            self.pending = values
            self.running = False


def release(*flows, ties=()):
    held = lax.optimization_barrier((tuple(flow.pending for flow in flows), ties))
    for flow, values in zip(flows, held[0]):
        flow.go(values)
    return held[1]


def finish(flow):
    while flow.running:
        release(flow)
    return flow.pending


def after(value, others):
    return lax.optimization_barrier((value, others))[0]


def pick(parts, at, axis):
    return lax.dynamic_index_in_dim(parts, at, axis, keepdims=False)


def by_core(core, own, other, axis):
    return jnp.where(
        core == 0, jnp.concatenate([own, other], axis), jnp.concatenate([other, own], axis)
    )


def normalize(rows):
    average = jnp.mean(rows, -1, keepdims=True)
    centered = rows - average
    scale = lax.rsqrt(jnp.mean(centered * centered, -1, keepdims=True) + EPS)
    return centered * scale, scale


def normalize_back(grads, normal, scale):
    return (
        grads
        - jnp.mean(grads, -1, keepdims=True)
        - normal * jnp.mean(grads * normal, -1, keepdims=True)
    ) * scale


def local(mesh):
    def run(
        layer_in, doc_ids, in_proj, out_proj, vec_bias, norm_gain, ffn_in, ffn_bias, ffn_out, out_grad
    ):
        links = Links(mesh)
        core, chips = links.core, links.chips
        side = (links.own // 2) % 2
        slots, shard, _ = layer_in.shape
        assert slots == 2 and mesh.shape["narrow"] == 4
        own_rows = in_proj.shape[1]
        chip_rows = 2 * own_rows
        hidden = ffn_out.shape[0]

        def halves(array):
            parts = array.reshape(array.shape[:-1] + (2, -1))
            return pick(parts, core, parts.ndim - 2), pick(parts, 1 - core, parts.ndim - 2)

        keep = pick(layer_in, side, 0)
        got_tokens = links.row_swap(pick(layer_in, 1 - side, 0))

        split = 3 * HALF
        trio_mine, trio_other = halves(in_proj)
        vectors = jnp.pad(jnp.concatenate([vec_bias, norm_gain], 0).T, ((0, 0), (0, SMALL - 8)))
        mine = jnp.concatenate([trio_mine[0], trio_mine[1], trio_mine[2], vectors], 1)
        other = jnp.concatenate([trio_other[0], trio_other[1], trio_other[2], vectors], 1)
        cols = by_core(core, mine, links.core_swap(other), 0)
        small = jnp.concatenate(
            [
                cols[:, split : split + 8],
                ffn_bias.reshape(chip_rows, 2),
                jnp.zeros((chip_rows, SMALL - 10), BF),
            ],
            1,
        )
        attn_block = jnp.concatenate([cols[:, :split], small], 1)
        attn = Flow(links.gather(attn_block, True, ((0, split), (split, split + SMALL))))
        (got_tokens,) = release(attn, ties=(got_tokens,))
        tokens = jnp.concatenate([keep, got_tokens], 0)
        down = Flow(links.gather(ffn_out, False))
        release(attn, down)
        release(attn)

        ffn_cols = ffn_in.reshape(own_rows, chips, 2, hidden).transpose(0, 2, 1, 3)
        ffn_cols = ffn_cols.reshape(own_rows, 2, chips * hidden)
        out_mine, out_other = halves(out_proj)
        mine = jnp.concatenate([pick(ffn_cols, core, 1), out_mine], 1)
        other = jnp.concatenate([pick(ffn_cols, 1 - core, 1), out_other], 1)
        cols = by_core(core, mine, links.core_swap(other), 0)
        up = Flow(links.gather(cols, True, ((0, FF // 2), (FF // 2, FF // 2 + HALF))))
        all_tokens = jnp.concatenate([tokens, links.core_swap(tokens)], 0)
        release(attn, up, down)
        (all_tokens,) = release(attn, up, down, ties=(all_tokens,))
        (all_tokens,) = release(up, ties=(all_tokens,))
        attn_pack = finish(attn)
        trio_weight = attn_pack[0].reshape(D, split)
        small = attn_pack[1]
        bias = small[..., :8].reshape(D, 8).T.astype(F32)
        up_bias = small[..., 8:10].reshape(FF // 2).astype(F32)

        slot_ids = pick(doc_ids, side, 0).reshape(2, 2, shard)
        slot_ids = jnp.stack(
            [
                slot_ids[side, core],
                slot_ids[1 - side, core],
                slot_ids[side, 1 - core],
                slot_ids[1 - side, 1 - core],
            ]
        )
        id_col = slot_ids.reshape(-1, 1)
        id_row = slot_ids.reshape(1, -1)
        low, high = jnp.min(slot_ids, 1), jnp.max(slot_ids, 1)

        own_bias = pick(bias[:2].reshape(2, 2, HALF), core, 1)
        zero = jnp.zeros_like(own_bias[0])
        trio_bias = jnp.concatenate([own_bias[0], zero, own_bias[1]])
        trio_scale = jnp.concatenate([zero + 0.125, zero + 1.0, zero + 1.0])
        trios = ((matmul(all_tokens, trio_weight) + trio_bias) * trio_scale).astype(BF)
        trios, row_grads = release(up, down, ties=(trios, out_grad))
        got_grads = links.row_swap(pick(row_grads, 1 - side, 0))
        mixed_heads, lse = attend(trios, low, high, id_col, id_row)
        up_weight, out_half = finish(up)
        up_weight = up_weight.reshape(D, FF // 2)
        out_half = out_half.reshape(D, HALF)
        out_weight = by_core(core, out_half, links.core_swap(out_half), 1)
        count = tokens.shape[0]
        mixed = by_core(core, mixed_heads[:count], links.core_swap(mixed_heads[count:]), 1)

        first_sum = tokens.astype(F32) + matmul(mixed, out_weight) + bias[2]
        first_normal, first_scale = normalize(first_sum)
        normed = first_normal * bias[6] + bias[3]
        normed_low = normed.astype(BF)
        all_normed = jnp.concatenate([normed_low, links.core_swap(normed_low)], 0)
        all_normed, got_grads = release(down, ties=(all_normed, got_grads))
        grad_out = jnp.concatenate([pick(row_grads, side, 0), got_grads], 0).astype(F32)
        down_weight = finish(down)[0][0]
        upper = matmul(all_normed, up_weight) + up_bias
        erf_part = 1.0 + lax.erf(upper * 0.7071067811865476)
        active = (0.5 * upper * erf_part).astype(BF)
        partial = matmul(active, down_weight)
        second_sum = (
            normed
            + partial[:count]
            + links.core_swap(partial[count:].astype(BF)).astype(F32)
            + bias[4]
        )
        second_normal, second_scale = normalize(second_sum)
        result = (second_normal * bias[7] + bias[5]).astype(BF)

        def home(rows):
            got = links.row_swap(rows[shard:])
            kept = rows[:shard]
            return jnp.where(side == 0, jnp.stack([kept, got]), jnp.stack([got, kept]))

        layer_out = home(result)

        grad_second = normalize_back(grad_out * bias[7], second_normal, second_scale)
        grad_down = grad_second.astype(BF)
        all_down = jnp.concatenate([grad_down, links.core_swap(grad_down)], 0)
        grad_down_weight = left_inner(active, all_down).astype(BF)
        grad_active = times_transposed(all_down, down_weight)
        slope = 0.5 * erf_part + upper * jnp.exp(-0.5 * upper * upper) * 0.3989422804014327
        grad_upper = (grad_active * slope).astype(BF)
        partial = times_transposed(grad_upper, up_weight)
        down_sum = Flow(links.scatter([grad_down_weight.reshape(chips, hidden, D)], True))
        (partial_got,) = release(down_sum, ties=(links.core_swap(partial[count:].astype(BF)),))
        grad_normed = grad_second + partial[:count] + partial_got.astype(F32)
        grad_up_weight = left_inner(all_normed, grad_upper).astype(BF)
        grad_first = normalize_back(grad_normed * bias[6], first_normal, first_scale)
        grad_attn = grad_first.astype(BF)
        grad_out_weight = left_inner(mixed, grad_attn).astype(BF)
        grad_mixed = times_transposed(grad_attn, out_weight).astype(BF)
        mine, other = halves(grad_mixed)
        grad_heads = jnp.concatenate([mine, links.core_swap(other)], 0)
        mine, other = halves(grad_out_weight)
        out_sum = (mine.astype(F32) + links.core_swap(other).astype(F32)).astype(BF)
        up_sum = Flow(
            links.scatter(
                [
                    grad_up_weight.reshape(chips, chip_rows, FF // 2),
                    out_sum.reshape(chips, chip_rows, HALF),
                ],
                False,
            )
        )
        (grad_heads,) = release(up_sum, ties=(grad_heads,))
        grad_trios = attend_back(trios, grad_heads, mixed_heads, low, high, id_col, id_row, lse)
        (grad_trios,) = release(down_sum, up_sum, ties=(grad_trios,))
        grad_trio_weight = left_inner(all_tokens, grad_trios).astype(BF)
        partial = times_transposed(grad_trios, trio_weight)
        grad_tokens = (
            grad_first
            + partial[:count]
            + links.core_swap(partial[count:].astype(BF)).astype(F32)
        )
        grad_in = home(grad_tokens.astype(BF))

        trio_sums = matmul(jnp.ones((8, grad_trios.shape[0]), BF), grad_trios)[0].reshape(3, HALF)
        own_half = jnp.stack([trio_sums[0], trio_sums[2]])
        none = jnp.zeros_like(own_half)
        sums = jnp.concatenate(
            [
                by_core(core, own_half, none, 1),
                jnp.stack(
                    [
                        jnp.sum(grad_attn.astype(F32), 0),
                        jnp.sum(grad_normed, 0),
                        jnp.sum(grad_down.astype(F32), 0),
                        jnp.sum(grad_out, 0),
                        jnp.sum(grad_normed * first_normal, 0),
                        jnp.sum(grad_out * second_normal, 0),
                    ]
                ),
            ],
            0,
        )
        up_bias_sum = jnp.sum(grad_upper.astype(F32), 0).reshape(chips, chip_rows, 2)
        small = jnp.concatenate(
            [
                sums.T.reshape(chips, chip_rows, 8),
                up_bias_sum,
                jnp.zeros((chips, chip_rows, SMALL - 10), F32),
            ],
            2,
        ).astype(BF)
        attn_sum = Flow(
            links.scatter([grad_trio_weight.reshape(chips, chip_rows, split), small], False)
        )
        release(attn_sum)
        release(down_sum, up_sum)
        release(attn_sum, down_sum, up_sum)
        release(attn_sum, down_sum, up_sum)
        release(attn_sum, down_sum, up_sum)
        down_total = finish(down_sum)[0]
        up_total = finish(up_sum)[0]
        attn_total = finish(attn_sum)[0]

        def both(array):
            rows = array.reshape(2, own_rows, -1)
            other = links.core_swap(pick(rows, 1 - core, 0).astype(BF))
            return pick(rows, core, 0), other.astype(F32)

        mine, got = both(up_total)
        grad_ffn_in = by_core(
            core,
            mine[:, : FF // 2].reshape(own_rows, chips, 1, hidden),
            got[:, : FF // 2].reshape(own_rows, chips, 1, hidden),
            2,
        ).reshape(own_rows, FF)
        grad_out_proj = by_core(core, mine[:, FF // 2 :], got[:, FF // 2 :], 1)
        mine, got = both(attn_total)
        grad_in_proj = jnp.stack(
            [
                by_core(core, mine[:, i * HALF : (i + 1) * HALF], got[:, i * HALF : (i + 1) * HALF], 1)
                for i in range(3)
            ]
        )
        vectors = (mine[:, split : split + 8] + got[:, split : split + 8]).T
        grad_ffn_bias = attn_total[:, split + 8 : split + 10].reshape(hidden)
        return (
            layer_out,
            grad_in,
            grad_in_proj,
            grad_out_proj,
            vectors[:6],
            vectors[6:],
            grad_ffn_in,
            grad_ffn_bias,
            down_total,
        )

    return run


def solution(mesh):
    return jax.shard_map(
        local(mesh),
        mesh=mesh,
        in_specs=(
            P("wide", "narrow", None),
            P("wide", None),
            P(None, AXES, None),
            P(AXES, None),
            P(None, AXES),
            P(None, AXES),
            P(AXES, None),
            P(AXES),
            P(AXES, None),
            P("wide", "narrow", None),
        ),
        out_specs=(
            P("wide", "narrow", None),
            P("wide", "narrow", None),
            P(None, AXES, None),
            P(AXES, None),
            P(None, AXES),
            P(None, AXES),
            P(AXES, None),
            P(AXES),
            P(AXES, None),
        ),
        check_vma=False,
    )
```

```python
import functools

import jax
import jax.numpy as jnp
from jax import lax
from jax.experimental import pallas as pl
from jax.experimental.pallas import tpu as pltpu
from jax.sharding import PartitionSpec as P

D = 768
FF = 3072
DH = 64
PAIR = 128
HALF = D // 2
QB = 256
AXES = ("wide", "narrow")
EPS = 1e-05
BF = jnp.bfloat16
F32 = jnp.float32
MASKED = -1000000000.0
SMALL = 128
BRIEF = pl.CostEstimate(flops=1000, transcendentals=0, bytes_accessed=1000)


def matmul(left, right):
    return jnp.dot(left, right, preferred_element_type=F32)


def times_transposed(left, right):
    return lax.dot_general(left, right, (((1,), (1,)), ((), ())), preferred_element_type=F32)


def left_inner(left, right):
    return lax.dot_general(left, right, (((0,), (0,)), ((), ())), preferred_element_type=F32)


def overlap(low_ref, high_ref, key_block, query_block):
    return (low_ref[key_block] <= high_ref[query_block]) & (
        low_ref[query_block] <= high_ref[key_block]
    )


def tile_ids(id_col_ref, id_row_ref, keys, queries):
    return id_col_ref[keys, :] == id_row_ref[:, queries]


def one_head(rows, head):
    lane = lax.broadcasted_iota(jnp.int32, rows.shape, 1)
    return jnp.where((lane < DH) if head % 2 == 0 else (lane >= DH), rows, jnp.zeros_like(rows))


def attend_kernel(
    low_ref, high_ref, trio_ref, id_col_ref, id_row_ref, mixed_ref, lse_ref, vt_ref, acc_ref, top_ref, mass_ref
):
    total = trio_ref.shape[0]
    heads = HALF // DH
    blocks = total // QB
    vt_ref[...] = trio_ref[:, 2 * HALF :].T
    acc_ref[...] = jnp.zeros_like(acc_ref)
    mass_ref[...] = jnp.zeros_like(mass_ref)
    top_ref[...] = jnp.full_like(top_ref, -jnp.inf)

    def tile(step, carry):
        query_block, key_block = step // blocks, step % blocks

        @pl.when(overlap(low_ref, high_ref, key_block, query_block))
        def _():
            queries = pl.ds(pl.multiple_of(query_block * QB, QB), QB)
            keys = pl.ds(pl.multiple_of(key_block * QB, QB), QB)
            same = tile_ids(id_col_ref, id_row_ref, keys, queries)
            old_tops = top_ref[:, queries]
            old_mass = mass_ref[:, queries]

            def score(head):
                lanes = slice(head // 2 * PAIR, head // 2 * PAIR + PAIR)
                q = one_head(trio_ref[queries, lanes], head)
                k = trio_ref[keys, HALF + lanes.start : HALF + lanes.stop]
                return jnp.where(same, times_transposed(k, q), MASKED)

            scores = [score(head) for head in range(heads)]
            tops = [jnp.maximum(old_tops[h : h + 1], jnp.max(scores[h], 0, keepdims=True)) for h in range(heads)]
            weights = [jnp.exp(scores[h] - tops[h]) for h in range(heads)]
            shrinks = [jnp.exp(old_tops[h : h + 1] - tops[h]) for h in range(heads)]
            masses = [old_mass[h : h + 1] * shrinks[h] + jnp.sum(weights[h], 0, keepdims=True) for h in range(heads)]
            outs = [matmul(vt_ref[h * DH : (h + 1) * DH, keys], weights[h].astype(BF)) for h in range(heads)]
            for h in range(heads):
                rows = slice(h * DH, (h + 1) * DH)
                acc_ref[rows, queries] = acc_ref[rows, queries] * shrinks[h] + outs[h]
            top_ref[:, queries] = jnp.concatenate(tops + [old_tops[heads:]], 0)
            mass_ref[:, queries] = jnp.concatenate(masses + [old_mass[heads:]], 0)

        return carry

    lax.fori_loop(0, blocks * blocks, tile, 0)
    for head in range(heads):
        rows = slice(head * DH, (head + 1) * DH)
        acc_ref[rows, :] = acc_ref[rows, :] / mass_ref[head : head + 1, :]
    mixed_ref[...] = acc_ref[...].T.astype(BF)
    lse_ref[...] = top_ref[...] + jnp.log(mass_ref[...])


def attend(trios, low, high, id_col, id_row):
    total, width = trios.shape
    return pl.pallas_call(
        attend_kernel,
        grid_spec=pltpu.PrefetchScalarGridSpec(
            num_scalar_prefetch=2,
            grid=(1,),
            in_specs=[
                pl.BlockSpec((total, width), lambda p, *_: (0, 0)),
                pl.BlockSpec((total, 1), lambda p, *_: (0, 0)),
                pl.BlockSpec((1, total), lambda p, *_: (0, 0)),
            ],
            out_specs=[
                pl.BlockSpec((total, HALF), lambda p, *_: (0, 0)),
                pl.BlockSpec((8, total), lambda p, *_: (0, 0)),
            ],
            scratch_shapes=[
                pltpu.VMEM((HALF, total), BF),
                pltpu.VMEM((HALF, total), F32),
                pltpu.VMEM((8, total), F32),
                pltpu.VMEM((8, total), F32),
            ],
        ),
        out_shape=[
            jax.ShapeDtypeStruct((total, HALF), BF),
            jax.ShapeDtypeStruct((8, total), F32),
        ],
        cost_estimate=BRIEF,
        name="attend",
    )(low, high, trios, id_col, id_row)


def attend_back_kernel(
    low_ref,
    high_ref,
    trio_ref,
    grad_ref,
    mixed_ref,
    id_col_ref,
    id_row_ref,
    lse_ref,
    out_ref,
    sums_ref,
    kt_ref,
    inner_ref,
    dq_ref,
    dk_ref,
    dv_ref,
):
    total = trio_ref.shape[0]
    heads = HALF // DH
    blocks = total // QB
    kt_ref[...] = trio_ref[:, HALF : 2 * HALF].T
    dq_ref[...] = jnp.zeros_like(dq_ref)
    dk_ref[...] = jnp.zeros_like(dk_ref)
    dv_ref[...] = jnp.zeros_like(dv_ref)
    lane = lax.broadcasted_iota(jnp.int32, (8, HALF), 1)
    row = lax.broadcasted_iota(jnp.int32, (8, HALF), 0)
    chosen = jnp.where(lane // DH == row, 1.0, 0.0)
    products = grad_ref[...].astype(F32) * mixed_ref[...].astype(F32)
    inner_ref[...] = lax.dot_general(
        chosen,
        products,
        (((1,), (1,)), ((), ())),
        precision=lax.Precision.HIGHEST,
        preferred_element_type=F32,
    )

    def tile(step, carry):
        query_block, key_block = step // blocks, step % blocks

        @pl.when(overlap(low_ref, high_ref, key_block, query_block))
        def _():
            queries = pl.ds(pl.multiple_of(query_block * QB, QB), QB)
            keys = pl.ds(pl.multiple_of(key_block * QB, QB), QB)
            same = tile_ids(id_col_ref, id_row_ref, keys, queries)
            tops = lse_ref[:, queries]
            inner = inner_ref[:, queries]
            q, k, v, g = [], [], [], []
            for head in range(heads):
                lanes = slice(head // 2 * PAIR, head // 2 * PAIR + PAIR)
                q.append(one_head(trio_ref[queries, lanes], head))
                g.append(one_head(grad_ref[queries, lanes], head))
                k.append(trio_ref[keys, HALF + lanes.start : HALF + lanes.stop])
                v.append(trio_ref[keys, 2 * HALF + lanes.start : 2 * HALF + lanes.stop])
            scores = [times_transposed(k[h], q[h]) for h in range(heads)]
            grad_probs = [times_transposed(v[h], g[h]) for h in range(heads)]
            probs = [jnp.where(same, jnp.exp(scores[h] - tops[h : h + 1]), 0.0) for h in range(heads)]
            grad_scores = [(probs[h] * (grad_probs[h] - inner[h : h + 1])).astype(BF) for h in range(heads)]
            probs = [probs[h].astype(BF) for h in range(heads)]
            dq = [matmul(kt_ref[h * DH : (h + 1) * DH, keys], grad_scores[h]) for h in range(heads)]
            dk = [matmul(grad_scores[h], q[h]) for h in range(heads)]
            dv = [matmul(probs[h], g[h]) for h in range(heads)]
            for h in range(heads):
                dq_ref[h * DH : (h + 1) * DH, queries] += dq[h]
            for pair in range(heads // 2):
                lanes = slice(pair * PAIR, pair * PAIR + PAIR)
                dk_ref[keys, lanes] += dk[2 * pair] + dk[2 * pair + 1]
                dv_ref[keys, lanes] += dv[2 * pair] + dv[2 * pair + 1]

        return carry

    lax.fori_loop(0, blocks * blocks, tile, 0)
    grads = (
        (dq_ref[...].T.astype(BF).astype(F32) * 0.125).astype(BF),
        dk_ref[...].astype(BF),
        dv_ref[...].astype(BF),
    )
    for part in range(3):
        lanes = slice(part * HALF, (part + 1) * HALF)
        out_ref[:, lanes] = grads[part]
        column = jnp.sum(grads[part].astype(F32), 0, keepdims=True)
        sums_ref[:, lanes] = jnp.broadcast_to(column, (8, HALF))


def attend_back(trios, grads, mixed, low, high, id_col, id_row, lse):
    total, width = trios.shape
    return pl.pallas_call(
        attend_back_kernel,
        grid_spec=pltpu.PrefetchScalarGridSpec(
            num_scalar_prefetch=2,
            grid=(1,),
            in_specs=[
                pl.BlockSpec((total, width), lambda p, *_: (0, 0)),
                pl.BlockSpec((total, HALF), lambda p, *_: (0, 0)),
                pl.BlockSpec((total, HALF), lambda p, *_: (0, 0)),
                pl.BlockSpec((total, 1), lambda p, *_: (0, 0)),
                pl.BlockSpec((1, total), lambda p, *_: (0, 0)),
                pl.BlockSpec((8, total), lambda p, *_: (0, 0)),
            ],
            out_specs=[
                pl.BlockSpec((total, width), lambda p, *_: (0, 0)),
                pl.BlockSpec((8, width), lambda p, *_: (0, 0)),
            ],
            scratch_shapes=[
                pltpu.VMEM((HALF, total), BF),
                pltpu.VMEM((8, total), F32),
                pltpu.VMEM((HALF, total), F32),
                pltpu.VMEM((total, HALF), F32),
                pltpu.VMEM((total, HALF), F32),
            ],
        ),
        out_shape=[
            jax.ShapeDtypeStruct((total, width), BF),
            jax.ShapeDtypeStruct((8, width), F32),
        ],
        cost_estimate=BRIEF,
        name="attend_back",
    )(low, high, trios, grads, mixed, id_col, id_row, lse)


def place_kernel(columns, index_ref, *refs):
    count = (len(refs) - 2 - len(columns)) // 2
    pieces, outs = refs[:count], refs[count : count + len(columns)]
    held = refs[count + len(columns) : -2]
    in_sem, out_sem = refs[-2:]
    arriving = [
        pltpu.make_async_copy(pieces[i], held[i], in_sem.at[i]) for i in range(count)
    ]
    for copy in arriving:
        copy.start()
    leaving = []
    for i in range(count):
        arriving[i].wait()
        for j, (start, stop) in enumerate(columns):
            copy = pltpu.make_async_copy(
                held[i].at[:, :, start:stop], outs[j].at[:, index_ref[i]], out_sem.at[i, j]
            )
            copy.start()
            leaving.append(copy)
    for copy in leaving:
        copy.wait()


def place(pieces, index, columns):
    count = len(pieces)
    outer, rows, _ = pieces[0].shape
    anywhere = pl.BlockSpec(memory_space=pl.ANY)
    return pl.pallas_call(
        functools.partial(place_kernel, columns),
        grid_spec=pltpu.PrefetchScalarGridSpec(
            num_scalar_prefetch=1,
            grid=(1,),
            in_specs=[anywhere] * count,
            out_specs=[anywhere] * len(columns),
            scratch_shapes=[pltpu.VMEM(piece.shape, piece.dtype) for piece in pieces]
            + [pltpu.SemaphoreType.DMA((count,)), pltpu.SemaphoreType.DMA((count, len(columns)))],
        ),
        out_shape=[
            jax.ShapeDtypeStruct((outer, count, rows, stop - start), pieces[0].dtype)
            for start, stop in columns
        ],
        cost_estimate=BRIEF,
        name="place",
    )(index, *pieces)


def take_kernel(columns, count, index_ref, *refs):
    arrays = refs[: len(columns)]
    outs = refs[len(columns) : len(columns) + count]
    held = refs[len(columns) + count : -2]
    in_sem, out_sem = refs[-2:]
    arriving = []
    for i in range(count):
        for j, (start, stop) in enumerate(columns):
            copy = pltpu.make_async_copy(
                arrays[j].at[:, index_ref[i]], held[i].at[:, :, start:stop], in_sem.at[i, j]
            )
            copy.start()
            arriving.append(copy)
    leaving = []
    for i in range(count):
        for copy in arriving[i * len(columns) : (i + 1) * len(columns)]:
            copy.wait()
        copy = pltpu.make_async_copy(held[i], outs[i], out_sem.at[i])
        copy.start()
        leaving.append(copy)
    for copy in leaving:
        copy.wait()


def take(arrays, index):
    outer, count, rows, _ = arrays[0].shape
    columns, start = [], 0
    for array in arrays:
        columns.append((start, start + array.shape[3]))
        start += array.shape[3]
    anywhere = pl.BlockSpec(memory_space=pl.ANY)
    return pl.pallas_call(
        functools.partial(take_kernel, tuple(columns), count),
        grid_spec=pltpu.PrefetchScalarGridSpec(
            num_scalar_prefetch=1,
            grid=(1,),
            in_specs=[anywhere] * len(arrays),
            out_specs=[anywhere] * count,
            scratch_shapes=[pltpu.VMEM((outer, rows, start), BF) for _ in range(count)]
            + [pltpu.SemaphoreType.DMA((count, len(arrays))), pltpu.SemaphoreType.DMA((count,))],
        ),
        out_shape=[jax.ShapeDtypeStruct((outer, rows, start), BF)] * count,
        cost_estimate=BRIEF,
        name="take",
    )(index, *arrays)


def weight_grad_kernel(outer, count, rows, index_ref, left_ref, right_ref, *refs):
    extra_ref = refs[0] if len(refs) > count + 1 else None
    outs, held_ref = refs[-1 - count : -1], refs[-1]
    width = right_ref.shape[1]
    held_ref[...] = left_inner(left_ref[...], right_ref[...]).astype(BF)
    for i in range(count):
        for part in range(outer):
            source = pl.ds(pl.multiple_of((part * count + index_ref[i]) * rows, 16), rows)
            outs[i][part, :, :width] = held_ref[source, :]
            if extra_ref is not None:
                outs[i][part, :, width:] = extra_ref[source, :]


def weight_grad(left, right, extra, index, count, rows):
    outer = left.shape[1] // (count * rows)
    arrays = [left, right] + ([] if extra is None else [extra])
    if rows % 16:
        wide = left_inner(left, right).astype(BF)
        wide = wide if extra is None else jnp.concatenate([wide, extra], 1)
        return take([wide.reshape(outer, count, rows, -1)], index)
    width = sum(array.shape[1] for array in arrays[1:])
    return pl.pallas_call(
        functools.partial(weight_grad_kernel, outer, count, rows),
        grid_spec=pltpu.PrefetchScalarGridSpec(
            num_scalar_prefetch=1,
            grid=(1,),
            in_specs=[pl.BlockSpec(array.shape, lambda p, *_: (0, 0)) for array in arrays],
            out_specs=[pl.BlockSpec((outer, rows, width), lambda p, *_: (0, 0, 0))] * count,
            scratch_shapes=[pltpu.VMEM((left.shape[1], right.shape[1]), BF)],
        ),
        out_shape=[jax.ShapeDtypeStruct((outer, rows, width), BF)] * count,
        cost_estimate=BRIEF,
        name="weight_grad",
    )(index, *arrays)


def sum_take_kernel(count, index_ref, *refs):
    arrays, outs = refs[:-count], refs[-count:]
    for i in range(count):
        total = arrays[0][:, index_ref[i]].astype(F32)
        for array in arrays[1:]:
            total += array[:, index_ref[i]].astype(F32)
        outs[i][...] = total.astype(BF)


def sum_take(arrays, index, count):
    arrays = [array.reshape((-1, count) + array.shape[1:]) for array in arrays]
    outer, _, rows, width = arrays[0].shape
    return pl.pallas_call(
        functools.partial(sum_take_kernel, count),
        grid_spec=pltpu.PrefetchScalarGridSpec(
            num_scalar_prefetch=1,
            grid=(1,),
            in_specs=[pl.BlockSpec(array.shape, lambda p, *_: (0, 0, 0, 0)) for array in arrays],
            out_specs=[pl.BlockSpec((outer, rows, width), lambda p, *_: (0, 0, 0))] * count,
        ),
        out_shape=[jax.ShapeDtypeStruct((outer, rows, width), BF)] * count,
        cost_estimate=BRIEF,
        name="sum_take",
    )(index, *arrays)


class Links:
    def __init__(self, mesh):
        self.devices = mesh.shape["wide"] * mesh.shape["narrow"]
        self.chips = self.devices // 2
        bits = self.chips.bit_length() - 1
        assert self.chips == 1 << bits
        self.groups = [(low, 2) for low in range(bits - 2, -1, -2)]
        if bits % 2:
            self.groups.append((0, 1))
        self.own = lax.axis_index(AXES)
        self.chip = self.own // 2
        self.core = self.own % 2

    def send(self, value, flip_even, flip_odd):
        pairs = [(d, d ^ (flip_odd if d % 2 else flip_even)) for d in range(self.devices)]
        return lax.ppermute(value, AXES, pairs)

    def core_swap(self, value):
        return self.send(value, 1, 1)

    def row_swap(self, value):
        return self.send(value, 2, 2)

    def spots(self, low, size):
        place = (self.chip >> low) % (1 << size)
        if size == 1:
            return jnp.stack([place, place ^ 1]).astype(jnp.int32)
        first, second = 1 + self.core, 2 - self.core
        return jnp.stack([place, place ^ first, place ^ second, place ^ 3]).astype(jnp.int32)

    def gather(self, block, high, columns=None):
        width = block.shape[1]
        have = block[None]
        groups = self.groups if high else self.groups[::-1]
        for stage, (low, size) in enumerate(groups):
            if size == 1:
                (one,) = yield (self.send(have, 2 << low, 2 << low),)
                yield ()
                pieces = [have, one]
            else:
                one = self.send(have, 2 << low, 4 << low)
                two = self.send(have, 4 << low, 2 << low)
                one, two = yield (one, two)
                (three,) = yield (self.send(one, 4 << low, 2 << low),)
                pieces = [have, one, two, three]
            last = stage == len(groups) - 1
            placed = place(pieces, self.spots(low, size), columns if last and columns else ((0, width),))
            if high:
                placed = [out.reshape((-1,) + out.shape[2:]) for out in placed]
            else:
                placed = [out.reshape(1, -1, out.shape[3]) for out in placed]
            placed = yield tuple(placed)
            have = placed[0]

    def scatter(self, left, right, extra=None):
        rows = left.shape[1] // self.chips
        for stage, (low, size) in enumerate(self.groups[::-1]):
            spots, count = self.spots(low, size), 1 << size
            if stage:
                pieces = sum_take(parts, spots, count)
            else:
                pieces = weight_grad(left, right, extra, spots, count, rows)
            pieces = yield tuple(pieces)
            if size == 1:
                (got,) = yield (self.send(pieces[1], 2 << low, 2 << low),)
                yield ()
                parts = [pieces[0], got]
            else:
                three = self.send(pieces[3], 4 << low, 2 << low)
                two = self.send(pieces[2], 4 << low, 2 << low)
                three, two = yield (three, two)
                one = (pieces[1].astype(F32) + three.astype(F32)).astype(BF)
                (one,) = yield (self.send(one, 2 << low, 4 << low),)
                parts = [pieces[0], two, one]
        yield (sum(part[0].astype(F32) for part in parts),)


class Flow:
    def __init__(self, steps):
        self.steps = steps
        self.pending = next(steps)
        self.running = True

    def go(self, values):
        try:
            self.pending = self.steps.send(values)
        except StopIteration:
            self.pending = values
            self.running = False


def release(*flows, ties=()):
    held = lax.optimization_barrier((tuple(flow.pending for flow in flows), ties))
    for flow, values in zip(flows, held[0]):
        flow.go(values)
    return held[1]


def finish(flow):
    while flow.running:
        release(flow)
    return flow.pending


def after(value, others):
    return lax.optimization_barrier((value, others))[0]


def pick(parts, at, axis):
    return lax.dynamic_index_in_dim(parts, at, axis, keepdims=False)


def by_core(core, own, other, axis):
    return jnp.where(
        core == 0, jnp.concatenate([own, other], axis), jnp.concatenate([other, own], axis)
    )


def normalize(rows):
    average = jnp.mean(rows, -1, keepdims=True)
    centered = rows - average
    scale = lax.rsqrt(jnp.mean(centered * centered, -1, keepdims=True) + EPS)
    return centered * scale, scale


def normalize_back(grads, normal, scale):
    return (
        grads
        - jnp.mean(grads, -1, keepdims=True)
        - normal * jnp.mean(grads * normal, -1, keepdims=True)
    ) * scale


def local(mesh):
    def run(
        layer_in, doc_ids, in_proj, out_proj, vec_bias, norm_gain, ffn_in, ffn_bias, ffn_out, out_grad
    ):
        links = Links(mesh)
        core, chips = links.core, links.chips
        side = (links.own // 2) % 2
        slots, shard, _ = layer_in.shape
        assert slots == 2 and mesh.shape["narrow"] == 4
        own_rows = in_proj.shape[1]
        chip_rows = 2 * own_rows
        hidden = ffn_out.shape[0]

        def halves(array):
            parts = array.reshape(array.shape[:-1] + (2, -1))
            return pick(parts, core, parts.ndim - 2), pick(parts, 1 - core, parts.ndim - 2)

        keep = pick(layer_in, side, 0)
        got_tokens = links.row_swap(pick(layer_in, 1 - side, 0))

        split = 3 * HALF
        trio_mine, trio_other = halves(in_proj)
        vectors = jnp.pad(jnp.concatenate([vec_bias, norm_gain], 0).T, ((0, 0), (0, SMALL - 8)))
        mine = jnp.concatenate([trio_mine[0], trio_mine[1], trio_mine[2], vectors], 1)
        other = jnp.concatenate([trio_other[0], trio_other[1], trio_other[2], vectors], 1)
        cols = by_core(core, mine, links.core_swap(other), 0)
        small = jnp.concatenate(
            [
                cols[:, split : split + 8],
                ffn_bias.reshape(chip_rows, 2),
                jnp.zeros((chip_rows, SMALL - 10), BF),
            ],
            1,
        )
        attn_block = jnp.concatenate([cols[:, :split], small], 1)
        attn = Flow(links.gather(attn_block, True, ((0, split), (split, split + SMALL))))
        down = Flow(links.gather(ffn_out, False))
        (got_tokens,) = release(attn, down, ties=(got_tokens,))
        tokens = jnp.concatenate([keep, got_tokens], 0)
        release(attn, down)
        release(attn)
        release(down)

        ffn_cols = ffn_in.reshape(own_rows, chips, 2, hidden).transpose(0, 2, 1, 3)
        ffn_cols = ffn_cols.reshape(own_rows, 2, chips * hidden)
        out_mine, out_other = halves(out_proj)
        mine = jnp.concatenate([pick(ffn_cols, core, 1), out_mine], 1)
        other = jnp.concatenate([pick(ffn_cols, 1 - core, 1), out_other], 1)
        cols = by_core(core, mine, links.core_swap(other), 0)
        up = Flow(links.gather(cols, True, ((0, FF // 2), (FF // 2, FF // 2 + HALF))))
        all_tokens = jnp.concatenate([tokens, links.core_swap(tokens)], 0)
        release(attn, up)
        (all_tokens,) = release(attn, up, ties=(all_tokens,))
        (all_tokens,) = release(up, ties=(all_tokens,))
        attn_pack = finish(attn)
        trio_weight = attn_pack[0].reshape(D, split)
        small = attn_pack[1]
        bias = small[..., :8].reshape(D, 8).T.astype(F32)
        up_bias = small[..., 8:10].reshape(FF // 2).astype(F32)

        slot_ids = pick(doc_ids, side, 0).reshape(2, 2, shard)
        slot_ids = jnp.stack(
            [
                slot_ids[side, core],
                slot_ids[1 - side, core],
                slot_ids[side, 1 - core],
                slot_ids[1 - side, 1 - core],
            ]
        )
        id_col = slot_ids.reshape(-1, 1)
        id_row = slot_ids.reshape(1, -1)
        low, high = jnp.min(slot_ids, 1), jnp.max(slot_ids, 1)

        own_bias = pick(bias[:2].reshape(2, 2, HALF), core, 1)
        zero = jnp.zeros_like(own_bias[0])
        trio_bias = jnp.concatenate([own_bias[0], zero, own_bias[1]])
        trio_scale = jnp.concatenate([zero + 0.125, zero + 1.0, zero + 1.0])
        trios = ((matmul(all_tokens, trio_weight) + trio_bias) * trio_scale).astype(BF)
        trios, row_grads = release(up, down, ties=(trios, out_grad))
        got_grads = links.row_swap(pick(row_grads, 1 - side, 0))
        mixed_heads, lse = attend(trios, low, high, id_col, id_row)
        mixed_heads, got_grads = release(up, down, ties=(mixed_heads, got_grads))
        grad_out = jnp.concatenate([pick(row_grads, side, 0), got_grads], 0).astype(F32)
        up_weight, out_half = finish(up)
        down_weight = finish(down)[0][0]
        up_weight = up_weight.reshape(D, FF // 2)
        out_half = out_half.reshape(D, HALF)
        out_weight = by_core(core, out_half, links.core_swap(out_half), 1)
        count = tokens.shape[0]
        mixed = by_core(core, mixed_heads[:count], links.core_swap(mixed_heads[count:]), 1)

        first_sum = tokens.astype(F32) + matmul(mixed, out_weight) + bias[2]
        first_normal, first_scale = normalize(first_sum)
        normed = first_normal * bias[6] + bias[3]
        normed_low = normed.astype(BF)
        all_normed = lax.optimization_barrier(
            jnp.concatenate([normed_low, links.core_swap(normed_low)], 0)
        )
        upper = matmul(all_normed, up_weight) + up_bias
        erf_part = 1.0 + lax.erf(upper * 0.7071067811865476)
        active = (0.5 * upper * erf_part).astype(BF)
        slope = 0.5 * erf_part + upper * jnp.exp(-0.5 * upper * upper) * 0.3989422804014327
        active, slope = lax.optimization_barrier((active, slope))
        partial = matmul(active, down_weight)
        second_sum = (
            normed
            + partial[:count]
            + links.core_swap(partial[count:].astype(BF)).astype(F32)
            + bias[4]
        )
        second_normal, second_scale = normalize(second_sum)
        result = (second_normal * bias[7] + bias[5]).astype(BF)

        def home(rows, got):
            kept = rows[:shard]
            return jnp.where(side == 0, jnp.stack([kept, got]), jnp.stack([got, kept]))

        got_result = links.row_swap(result[shard:])

        grad_second = normalize_back(grad_out * bias[7], second_normal, second_scale)
        grad_down = grad_second.astype(BF)
        all_down = lax.optimization_barrier(
            jnp.concatenate([grad_down, links.core_swap(grad_down)], 0)
        )
        grad_active = times_transposed(all_down, down_weight)
        grad_upper = (grad_active * slope).astype(BF)
        partial = times_transposed(grad_upper, up_weight)
        down_sum = Flow(links.scatter(active, all_down))
        (partial_got,) = release(down_sum, ties=(links.core_swap(partial[count:].astype(BF)),))
        grad_normed = grad_second + partial[:count] + partial_got.astype(F32)
        (grad_upper,) = release(down_sum, ties=(grad_upper,))
        grad_first = normalize_back(grad_normed * bias[6], first_normal, first_scale)
        grad_attn = grad_first.astype(BF)
        grad_out_weight = left_inner(mixed, grad_attn).astype(BF)
        grad_mixed = times_transposed(grad_attn, out_weight).astype(BF)
        mine, other = halves(grad_mixed)
        grad_heads = jnp.concatenate([mine, links.core_swap(other)], 0)
        mine, other = halves(grad_out_weight)
        out_sum = (mine.astype(F32) + links.core_swap(other).astype(F32)).astype(BF)
        up_sum = Flow(links.scatter(all_normed, grad_upper, out_sum))
        (grad_heads,) = release(down_sum, up_sum, ties=(grad_heads,))
        (grad_heads,) = release(down_sum, ties=(grad_heads,))
        grad_trios, trio_sums = attend_back(
            trios, grad_heads, mixed_heads, low, high, id_col, id_row, lse
        )
        trio_sums = trio_sums[0].reshape(3, HALF)

        own_half = jnp.stack([trio_sums[0], trio_sums[2]])
        none = jnp.zeros_like(own_half)
        sums = jnp.concatenate(
            [
                by_core(core, own_half, none, 1),
                jnp.stack(
                    [
                        jnp.sum(grad_attn.astype(F32), 0),
                        jnp.sum(grad_normed, 0),
                        jnp.sum(grad_down.astype(F32), 0),
                        jnp.sum(grad_out, 0),
                        jnp.sum(grad_normed * first_normal, 0),
                        jnp.sum(grad_out * second_normal, 0),
                    ]
                ),
            ],
            0,
        )
        up_bias_sum = jnp.sum(grad_upper.astype(F32), 0).reshape(D, 2)
        small = jnp.concatenate(
            [sums.T, up_bias_sum, jnp.zeros((D, SMALL - 10), F32)], 1
        ).astype(BF)
        attn_sum = Flow(links.scatter(all_tokens, grad_trios, small))
        grad_trios, got_result = release(
            attn_sum, down_sum, up_sum, ties=(grad_trios, got_result)
        )
        layer_out = home(result, got_result)
        partial = times_transposed(grad_trios, trio_weight)
        grad_tokens = (
            grad_first
            + partial[:count]
            + links.core_swap(partial[count:].astype(BF)).astype(F32)
        )
        grad_tokens = grad_tokens.astype(BF)
        grad_in = home(grad_tokens, links.row_swap(grad_tokens[shard:]))

        release(attn_sum, down_sum, up_sum)
        release(up_sum)
        release(attn_sum)
        release(attn_sum)
        release(attn_sum, up_sum)
        down_total = finish(down_sum)[0]
        up_total = finish(up_sum)[0]
        attn_total = finish(attn_sum)[0]

        def both(array):
            rows = array.reshape(2, own_rows, -1)
            other = links.core_swap(pick(rows, 1 - core, 0).astype(BF))
            return pick(rows, core, 0), other.astype(F32)

        mine, got = both(up_total)
        grad_ffn_in = by_core(
            core,
            mine[:, : FF // 2].reshape(own_rows, chips, 1, hidden),
            got[:, : FF // 2].reshape(own_rows, chips, 1, hidden),
            2,
        ).reshape(own_rows, FF)
        grad_out_proj = by_core(core, mine[:, FF // 2 :], got[:, FF // 2 :], 1)
        mine, got = both(attn_total)
        grad_in_proj = jnp.stack(
            [
                by_core(core, mine[:, i * HALF : (i + 1) * HALF], got[:, i * HALF : (i + 1) * HALF], 1)
                for i in range(3)
            ]
        )
        vectors = (mine[:, split : split + 8] + got[:, split : split + 8]).T
        grad_ffn_bias = attn_total[:, split + 8 : split + 10].reshape(hidden)
        return (
            layer_out,
            grad_in,
            grad_in_proj,
            grad_out_proj,
            vectors[:6],
            vectors[6:],
            grad_ffn_in,
            grad_ffn_bias,
            down_total,
        )

    return run


def solution(mesh):
    return jax.shard_map(
        local(mesh),
        mesh=mesh,
        in_specs=(
            P("wide", "narrow", None),
            P("wide", None),
            P(None, AXES, None),
            P(AXES, None),
            P(None, AXES),
            P(None, AXES),
            P(AXES, None),
            P(AXES),
            P(AXES, None),
            P("wide", "narrow", None),
        ),
        out_specs=(
            P("wide", "narrow", None),
            P("wide", "narrow", None),
            P(None, AXES, None),
            P(AXES, None),
            P(None, AXES),
            P(None, AXES),
            P(AXES, None),
            P(AXES),
            P(AXES, None),
        ),
        check_vma=False,
    )
```

```python
import functools

import jax
import jax.numpy as jnp
from jax import lax
from jax.experimental import pallas as pl
from jax.experimental.pallas import tpu as pltpu
from jax.sharding import PartitionSpec as P

D = 768
FF = 3072
DH = 64
PAIR = 128
HALF = D // 2
QB = 256
AXES = ("wide", "narrow")
EPS = 1e-05
BF = jnp.bfloat16
F32 = jnp.float32
MASKED = -1000000000.0
SMALL = 128
BRIEF = pl.CostEstimate(flops=1000, transcendentals=0, bytes_accessed=1000)


def matmul(left, right):
    return jnp.dot(left, right, preferred_element_type=F32)


def times_transposed(left, right):
    return lax.dot_general(left, right, (((1,), (1,)), ((), ())), preferred_element_type=F32)


def left_inner(left, right):
    return lax.dot_general(left, right, (((0,), (0,)), ((), ())), preferred_element_type=F32)


def overlap(low_ref, high_ref, key_block, query_block):
    return (low_ref[key_block] <= high_ref[query_block]) & (
        low_ref[query_block] <= high_ref[key_block]
    )


def tile_ids(id_col_ref, id_row_ref, keys, queries):
    return id_col_ref[keys, :] == id_row_ref[:, queries]


def one_head(rows, head):
    lane = lax.broadcasted_iota(jnp.int32, rows.shape, 1)
    return jnp.where((lane < DH) if head % 2 == 0 else (lane >= DH), rows, jnp.zeros_like(rows))


def attend_kernel(
    low_ref, high_ref, trio_ref, id_col_ref, id_row_ref, mixed_ref, lse_ref, vt_ref, acc_ref, top_ref, mass_ref
):
    total = trio_ref.shape[0]
    heads = HALF // DH
    blocks = total // QB
    vt_ref[...] = trio_ref[:, 2 * HALF :].T
    acc_ref[...] = jnp.zeros_like(acc_ref)
    mass_ref[...] = jnp.zeros_like(mass_ref)
    top_ref[...] = jnp.full_like(top_ref, -jnp.inf)

    def tile(step, carry):
        query_block, key_block = step // blocks, step % blocks

        @pl.when(overlap(low_ref, high_ref, key_block, query_block))
        def _():
            queries = pl.ds(pl.multiple_of(query_block * QB, QB), QB)
            keys = pl.ds(pl.multiple_of(key_block * QB, QB), QB)
            same = tile_ids(id_col_ref, id_row_ref, keys, queries)
            old_tops = top_ref[:, queries]
            old_mass = mass_ref[:, queries]

            def score(head):
                lanes = slice(head // 2 * PAIR, head // 2 * PAIR + PAIR)
                q = one_head(trio_ref[queries, lanes], head)
                k = trio_ref[keys, HALF + lanes.start : HALF + lanes.stop]
                return jnp.where(same, times_transposed(k, q), MASKED)

            scores = [score(head) for head in range(heads)]
            tops = [jnp.maximum(old_tops[h : h + 1], jnp.max(scores[h], 0, keepdims=True)) for h in range(heads)]
            weights = [jnp.exp(scores[h] - tops[h]) for h in range(heads)]
            shrinks = [jnp.exp(old_tops[h : h + 1] - tops[h]) for h in range(heads)]
            masses = [old_mass[h : h + 1] * shrinks[h] + jnp.sum(weights[h], 0, keepdims=True) for h in range(heads)]
            outs = [matmul(vt_ref[h * DH : (h + 1) * DH, keys], weights[h].astype(BF)) for h in range(heads)]
            for h in range(heads):
                rows = slice(h * DH, (h + 1) * DH)
                acc_ref[rows, queries] = acc_ref[rows, queries] * shrinks[h] + outs[h]
            top_ref[:, queries] = jnp.concatenate(tops + [old_tops[heads:]], 0)
            mass_ref[:, queries] = jnp.concatenate(masses + [old_mass[heads:]], 0)

        return carry

    lax.fori_loop(0, blocks * blocks, tile, 0)
    for head in range(heads):
        rows = slice(head * DH, (head + 1) * DH)
        acc_ref[rows, :] = acc_ref[rows, :] / mass_ref[head : head + 1, :]
    mixed_ref[...] = acc_ref[...].T.astype(BF)
    lse_ref[...] = top_ref[...] + jnp.log(mass_ref[...])


def attend(trios, low, high, id_col, id_row):
    total, width = trios.shape
    return pl.pallas_call(
        attend_kernel,
        grid_spec=pltpu.PrefetchScalarGridSpec(
            num_scalar_prefetch=2,
            grid=(1,),
            in_specs=[
                pl.BlockSpec((total, width), lambda p, *_: (0, 0)),
                pl.BlockSpec((total, 1), lambda p, *_: (0, 0)),
                pl.BlockSpec((1, total), lambda p, *_: (0, 0)),
            ],
            out_specs=[
                pl.BlockSpec((total, HALF), lambda p, *_: (0, 0)),
                pl.BlockSpec((8, total), lambda p, *_: (0, 0)),
            ],
            scratch_shapes=[
                pltpu.VMEM((HALF, total), BF),
                pltpu.VMEM((HALF, total), F32),
                pltpu.VMEM((8, total), F32),
                pltpu.VMEM((8, total), F32),
            ],
        ),
        out_shape=[
            jax.ShapeDtypeStruct((total, HALF), BF),
            jax.ShapeDtypeStruct((8, total), F32),
        ],
        cost_estimate=BRIEF,
        name="attend",
    )(low, high, trios, id_col, id_row)


def attend_back_kernel(
    low_ref,
    high_ref,
    trio_ref,
    grad_ref,
    mixed_ref,
    id_col_ref,
    id_row_ref,
    lse_ref,
    out_ref,
    sums_ref,
    kt_ref,
    inner_ref,
    dq_ref,
    dk_ref,
    dv_ref,
):
    total = trio_ref.shape[0]
    heads = HALF // DH
    blocks = total // QB
    kt_ref[...] = trio_ref[:, HALF : 2 * HALF].T
    dq_ref[...] = jnp.zeros_like(dq_ref)
    dk_ref[...] = jnp.zeros_like(dk_ref)
    dv_ref[...] = jnp.zeros_like(dv_ref)
    lane = lax.broadcasted_iota(jnp.int32, (8, HALF), 1)
    row = lax.broadcasted_iota(jnp.int32, (8, HALF), 0)
    chosen = jnp.where(lane // DH == row, 1.0, 0.0)
    products = grad_ref[...].astype(F32) * mixed_ref[...].astype(F32)
    inner_ref[...] = lax.dot_general(
        chosen,
        products,
        (((1,), (1,)), ((), ())),
        precision=lax.Precision.HIGHEST,
        preferred_element_type=F32,
    )

    def tile(step, carry):
        query_block, key_block = step // blocks, step % blocks

        @pl.when(overlap(low_ref, high_ref, key_block, query_block))
        def _():
            queries = pl.ds(pl.multiple_of(query_block * QB, QB), QB)
            keys = pl.ds(pl.multiple_of(key_block * QB, QB), QB)
            same = tile_ids(id_col_ref, id_row_ref, keys, queries)
            tops = lse_ref[:, queries]
            inner = inner_ref[:, queries]
            q, k, v, g = [], [], [], []
            for head in range(heads):
                lanes = slice(head // 2 * PAIR, head // 2 * PAIR + PAIR)
                q.append(one_head(trio_ref[queries, lanes], head))
                g.append(one_head(grad_ref[queries, lanes], head))
                k.append(trio_ref[keys, HALF + lanes.start : HALF + lanes.stop])
                v.append(trio_ref[keys, 2 * HALF + lanes.start : 2 * HALF + lanes.stop])
            scores = [times_transposed(k[h], q[h]) for h in range(heads)]
            grad_probs = [times_transposed(v[h], g[h]) for h in range(heads)]
            probs = [jnp.where(same, jnp.exp(scores[h] - tops[h : h + 1]), 0.0) for h in range(heads)]
            grad_scores = [(probs[h] * (grad_probs[h] - inner[h : h + 1])).astype(BF) for h in range(heads)]
            probs = [probs[h].astype(BF) for h in range(heads)]
            dq = [matmul(kt_ref[h * DH : (h + 1) * DH, keys], grad_scores[h]) for h in range(heads)]
            dk = [matmul(grad_scores[h], q[h]) for h in range(heads)]
            dv = [matmul(probs[h], g[h]) for h in range(heads)]
            for h in range(heads):
                dq_ref[h * DH : (h + 1) * DH, queries] += dq[h]
            for pair in range(heads // 2):
                lanes = slice(pair * PAIR, pair * PAIR + PAIR)
                dk_ref[keys, lanes] += dk[2 * pair] + dk[2 * pair + 1]
                dv_ref[keys, lanes] += dv[2 * pair] + dv[2 * pair + 1]

        return carry

    lax.fori_loop(0, blocks * blocks, tile, 0)
    grads = (
        (dq_ref[...].T.astype(BF).astype(F32) * 0.125).astype(BF),
        dk_ref[...].astype(BF),
        dv_ref[...].astype(BF),
    )
    for part in range(3):
        lanes = slice(part * HALF, (part + 1) * HALF)
        out_ref[:, lanes] = grads[part]
        column = jnp.sum(grads[part].astype(F32), 0, keepdims=True)
        sums_ref[:, lanes] = jnp.broadcast_to(column, (8, HALF))


def attend_back(trios, grads, mixed, low, high, id_col, id_row, lse):
    total, width = trios.shape
    return pl.pallas_call(
        attend_back_kernel,
        grid_spec=pltpu.PrefetchScalarGridSpec(
            num_scalar_prefetch=2,
            grid=(1,),
            in_specs=[
                pl.BlockSpec((total, width), lambda p, *_: (0, 0)),
                pl.BlockSpec((total, HALF), lambda p, *_: (0, 0)),
                pl.BlockSpec((total, HALF), lambda p, *_: (0, 0)),
                pl.BlockSpec((total, 1), lambda p, *_: (0, 0)),
                pl.BlockSpec((1, total), lambda p, *_: (0, 0)),
                pl.BlockSpec((8, total), lambda p, *_: (0, 0)),
            ],
            out_specs=[
                pl.BlockSpec((total, width), lambda p, *_: (0, 0)),
                pl.BlockSpec((8, width), lambda p, *_: (0, 0)),
            ],
            scratch_shapes=[
                pltpu.VMEM((HALF, total), BF),
                pltpu.VMEM((8, total), F32),
                pltpu.VMEM((HALF, total), F32),
                pltpu.VMEM((total, HALF), F32),
                pltpu.VMEM((total, HALF), F32),
            ],
        ),
        out_shape=[
            jax.ShapeDtypeStruct((total, width), BF),
            jax.ShapeDtypeStruct((8, width), F32),
        ],
        cost_estimate=BRIEF,
        name="attend_back",
    )(low, high, trios, grads, mixed, id_col, id_row, lse)


def place_kernel(columns, index_ref, *refs):
    count = (len(refs) - 2 - len(columns)) // 2
    pieces, outs = refs[:count], refs[count : count + len(columns)]
    held = refs[count + len(columns) : -2]
    in_sem, out_sem = refs[-2:]
    arriving = [
        pltpu.make_async_copy(pieces[i], held[i], in_sem.at[i]) for i in range(count)
    ]
    for copy in arriving:
        copy.start()
    leaving = []
    for i in range(count):
        arriving[i].wait()
        for j, (start, stop) in enumerate(columns):
            copy = pltpu.make_async_copy(
                held[i].at[:, :, start:stop], outs[j].at[:, index_ref[i]], out_sem.at[i, j]
            )
            copy.start()
            leaving.append(copy)
    for copy in leaving:
        copy.wait()


def place(pieces, index, columns):
    count = len(pieces)
    outer, rows, _ = pieces[0].shape
    anywhere = pl.BlockSpec(memory_space=pl.ANY)
    return pl.pallas_call(
        functools.partial(place_kernel, columns),
        grid_spec=pltpu.PrefetchScalarGridSpec(
            num_scalar_prefetch=1,
            grid=(1,),
            in_specs=[anywhere] * count,
            out_specs=[anywhere] * len(columns),
            scratch_shapes=[pltpu.VMEM(piece.shape, piece.dtype) for piece in pieces]
            + [pltpu.SemaphoreType.DMA((count,)), pltpu.SemaphoreType.DMA((count, len(columns)))],
        ),
        out_shape=[
            jax.ShapeDtypeStruct((outer, count, rows, stop - start), pieces[0].dtype)
            for start, stop in columns
        ],
        cost_estimate=BRIEF,
        name="place",
    )(index, *pieces)


def take_kernel(columns, count, index_ref, *refs):
    arrays = refs[: len(columns)]
    outs = refs[len(columns) : len(columns) + count]
    held = refs[len(columns) + count : -2]
    in_sem, out_sem = refs[-2:]
    arriving = []
    for i in range(count):
        for j, (start, stop) in enumerate(columns):
            copy = pltpu.make_async_copy(
                arrays[j].at[:, index_ref[i]], held[i].at[:, :, start:stop], in_sem.at[i, j]
            )
            copy.start()
            arriving.append(copy)
    leaving = []
    for i in range(count):
        for copy in arriving[i * len(columns) : (i + 1) * len(columns)]:
            copy.wait()
        copy = pltpu.make_async_copy(held[i], outs[i], out_sem.at[i])
        copy.start()
        leaving.append(copy)
    for copy in leaving:
        copy.wait()


def take(arrays, index):
    outer, count, rows, _ = arrays[0].shape
    columns, start = [], 0
    for array in arrays:
        columns.append((start, start + array.shape[3]))
        start += array.shape[3]
    anywhere = pl.BlockSpec(memory_space=pl.ANY)
    return pl.pallas_call(
        functools.partial(take_kernel, tuple(columns), count),
        grid_spec=pltpu.PrefetchScalarGridSpec(
            num_scalar_prefetch=1,
            grid=(1,),
            in_specs=[anywhere] * len(arrays),
            out_specs=[anywhere] * count,
            scratch_shapes=[pltpu.VMEM((outer, rows, start), BF) for _ in range(count)]
            + [pltpu.SemaphoreType.DMA((count, len(arrays))), pltpu.SemaphoreType.DMA((count,))],
        ),
        out_shape=[jax.ShapeDtypeStruct((outer, rows, start), BF)] * count,
        cost_estimate=BRIEF,
        name="take",
    )(index, *arrays)


def weight_grad_kernel(outer, count, rows, index_ref, left_ref, right_ref, *refs):
    extra_ref = refs[0] if len(refs) > count + 1 else None
    outs, held_ref = refs[-1 - count : -1], refs[-1]
    width = right_ref.shape[1]
    held_ref[...] = left_inner(left_ref[...], right_ref[...]).astype(BF)
    for i in range(count):
        for part in range(outer):
            source = pl.ds(pl.multiple_of((part * count + index_ref[i]) * rows, 16), rows)
            outs[i][part, :, :width] = held_ref[source, :]
            if extra_ref is not None:
                outs[i][part, :, width:] = extra_ref[source, :]


def weight_grad(left, right, extra, index, count, rows):
    outer = left.shape[1] // (count * rows)
    arrays = [left, right] + ([] if extra is None else [extra])
    if rows % 16:
        wide = left_inner(left, right).astype(BF)
        wide = wide if extra is None else jnp.concatenate([wide, extra], 1)
        return take([wide.reshape(outer, count, rows, -1)], index)
    width = sum(array.shape[1] for array in arrays[1:])
    return pl.pallas_call(
        functools.partial(weight_grad_kernel, outer, count, rows),
        grid_spec=pltpu.PrefetchScalarGridSpec(
            num_scalar_prefetch=1,
            grid=(1,),
            in_specs=[pl.BlockSpec(array.shape, lambda p, *_: (0, 0)) for array in arrays],
            out_specs=[pl.BlockSpec((outer, rows, width), lambda p, *_: (0, 0, 0))] * count,
            scratch_shapes=[pltpu.VMEM((left.shape[1], right.shape[1]), BF)],
        ),
        out_shape=[jax.ShapeDtypeStruct((outer, rows, width), BF)] * count,
        cost_estimate=BRIEF,
        name="weight_grad",
    )(index, *arrays)


def hidden_back_kernel(own_steps, rows_ref, down_ref, slope_ref, up_ref, grad_ref, own_ref, other_ref):
    grad = (times_transposed(rows_ref[...], down_ref[...]) * slope_ref[...]).astype(BF)
    grad_ref[...] = grad
    partial = times_transposed(grad, up_ref[...])

    @pl.when(pl.program_id(0) < own_steps)
    def _():
        own_ref[...] = partial

    @pl.when(pl.program_id(0) >= own_steps)
    def _():
        other_ref[...] = partial.astype(BF)


def hidden_back(rows, down, slope, up):
    total, width = rows.shape
    units = slope.shape[1]
    block = 256 if total % 512 == 0 else total // 2
    own_steps = total // 2 // block
    return pl.pallas_call(
        functools.partial(hidden_back_kernel, own_steps),
        grid=(total // block,),
        in_specs=[
            pl.BlockSpec((block, width), lambda i: (i, 0)),
            pl.BlockSpec((units, width), lambda i: (0, 0), pipeline_mode=pl.Buffered(1)),
            pl.BlockSpec((block, units), lambda i: (i, 0)),
            pl.BlockSpec((width, units), lambda i: (0, 0), pipeline_mode=pl.Buffered(1)),
        ],
        out_specs=[
            pl.BlockSpec((block, units), lambda i: (i, 0)),
            pl.BlockSpec((block, width), lambda i: (jnp.minimum(i, own_steps - 1), 0)),
            pl.BlockSpec((block, width), lambda i: (jnp.maximum(i - own_steps, 0), 0)),
        ],
        out_shape=[
            jax.ShapeDtypeStruct((total, units), BF),
            jax.ShapeDtypeStruct((total // 2, width), F32),
            jax.ShapeDtypeStruct((total // 2, width), BF),
        ],
        cost_estimate=BRIEF,
        name="hidden_back",
    )(rows, down, slope, up)


def sum_take_kernel(count, index_ref, *refs):
    arrays, outs = refs[:-count], refs[-count:]
    for i in range(count):
        total = arrays[0][:, index_ref[i]].astype(F32)
        for array in arrays[1:]:
            total += array[:, index_ref[i]].astype(F32)
        outs[i][...] = total.astype(BF)


def sum_take(arrays, index, count):
    arrays = [array.reshape((-1, count) + array.shape[1:]) for array in arrays]
    outer, _, rows, width = arrays[0].shape
    return pl.pallas_call(
        functools.partial(sum_take_kernel, count),
        grid_spec=pltpu.PrefetchScalarGridSpec(
            num_scalar_prefetch=1,
            grid=(1,),
            in_specs=[pl.BlockSpec(array.shape, lambda p, *_: (0, 0, 0, 0)) for array in arrays],
            out_specs=[pl.BlockSpec((outer, rows, width), lambda p, *_: (0, 0, 0))] * count,
        ),
        out_shape=[jax.ShapeDtypeStruct((outer, rows, width), BF)] * count,
        cost_estimate=BRIEF,
        name="sum_take",
    )(index, *arrays)


class Links:
    def __init__(self, mesh):
        self.devices = mesh.shape["wide"] * mesh.shape["narrow"]
        self.chips = self.devices // 2
        bits = self.chips.bit_length() - 1
        assert self.chips == 1 << bits
        self.groups = [(low, 2) for low in range(bits - 2, -1, -2)]
        if bits % 2:
            self.groups.append((0, 1))
        self.own = lax.axis_index(AXES)
        self.chip = self.own // 2
        self.core = self.own % 2

    def send(self, value, flip_even, flip_odd):
        pairs = [(d, d ^ (flip_odd if d % 2 else flip_even)) for d in range(self.devices)]
        return lax.ppermute(value, AXES, pairs)

    def core_swap(self, value):
        return self.send(value, 1, 1)

    def row_swap(self, value):
        return self.send(value, 2, 2)

    def spots(self, low, size):
        place = (self.chip >> low) % (1 << size)
        if size == 1:
            return jnp.stack([place, place ^ 1]).astype(jnp.int32)
        first, second = 1 + self.core, 2 - self.core
        return jnp.stack([place, place ^ first, place ^ second, place ^ 3]).astype(jnp.int32)

    def gather(self, block, high, columns=None):
        width = block.shape[1]
        have = block[None]
        groups = self.groups if high else self.groups[::-1]
        for stage, (low, size) in enumerate(groups):
            if size == 1:
                (one,) = yield (self.send(have, 2 << low, 2 << low),)
                yield ()
                pieces = [have, one]
            else:
                one = self.send(have, 2 << low, 4 << low)
                two = self.send(have, 4 << low, 2 << low)
                one, two = yield (one, two)
                (three,) = yield (self.send(one, 4 << low, 2 << low),)
                pieces = [have, one, two, three]
            last = stage == len(groups) - 1
            placed = place(pieces, self.spots(low, size), columns if last and columns else ((0, width),))
            if high:
                placed = [out.reshape((-1,) + out.shape[2:]) for out in placed]
            else:
                placed = [out.reshape(1, -1, out.shape[3]) for out in placed]
            placed = yield tuple(placed)
            have = placed[0]

    def scatter(self, left, right, extra=None):
        rows = left.shape[1] // self.chips
        for stage, (low, size) in enumerate(self.groups[::-1]):
            spots, count = self.spots(low, size), 1 << size
            if stage:
                pieces = sum_take(parts, spots, count)
            else:
                pieces = weight_grad(left, right, extra, spots, count, rows)
            pieces = yield tuple(pieces)
            if size == 1:
                (got,) = yield (self.send(pieces[1], 2 << low, 2 << low),)
                yield ()
                parts = [pieces[0], got]
            else:
                three = self.send(pieces[3], 4 << low, 2 << low)
                two = self.send(pieces[2], 4 << low, 2 << low)
                three, two = yield (three, two)
                one = (pieces[1].astype(F32) + three.astype(F32)).astype(BF)
                (one,) = yield (self.send(one, 2 << low, 4 << low),)
                parts = [pieces[0], two, one]
        yield (sum(part[0].astype(F32) for part in parts),)


class Flow:
    def __init__(self, steps):
        self.steps = steps
        self.pending = next(steps)
        self.running = True

    def go(self, values):
        try:
            self.pending = self.steps.send(values)
        except StopIteration:
            self.pending = values
            self.running = False


def release(*flows, ties=()):
    held = lax.optimization_barrier((tuple(flow.pending for flow in flows), ties))
    for flow, values in zip(flows, held[0]):
        flow.go(values)
    return held[1]


def finish(flow):
    while flow.running:
        release(flow)
    return flow.pending


def after(value, others):
    return lax.optimization_barrier((value, others))[0]


def pick(parts, at, axis):
    return lax.dynamic_index_in_dim(parts, at, axis, keepdims=False)


def by_core(core, own, other, axis):
    return jnp.where(
        core == 0, jnp.concatenate([own, other], axis), jnp.concatenate([other, own], axis)
    )


def normalize(rows):
    average = jnp.mean(rows, -1, keepdims=True)
    centered = rows - average
    scale = lax.rsqrt(jnp.mean(centered * centered, -1, keepdims=True) + EPS)
    return centered * scale, scale


def normalize_back(grads, normal, scale):
    return (
        grads
        - jnp.mean(grads, -1, keepdims=True)
        - normal * jnp.mean(grads * normal, -1, keepdims=True)
    ) * scale


def local(mesh):
    def run(
        layer_in, doc_ids, in_proj, out_proj, vec_bias, norm_gain, ffn_in, ffn_bias, ffn_out, out_grad
    ):
        links = Links(mesh)
        core, chips = links.core, links.chips
        side = (links.own // 2) % 2
        slots, shard, _ = layer_in.shape
        assert slots == 2 and mesh.shape["narrow"] == 4
        own_rows = in_proj.shape[1]
        chip_rows = 2 * own_rows
        hidden = ffn_out.shape[0]

        def halves(array):
            parts = array.reshape(array.shape[:-1] + (2, -1))
            return pick(parts, core, parts.ndim - 2), pick(parts, 1 - core, parts.ndim - 2)

        keep = pick(layer_in, side, 0)
        got_tokens = links.row_swap(pick(layer_in, 1 - side, 0))

        split = 3 * HALF
        trio_mine, trio_other = halves(in_proj)
        vectors = jnp.pad(jnp.concatenate([vec_bias, norm_gain], 0).T, ((0, 0), (0, SMALL - 8)))
        mine = jnp.concatenate([trio_mine[0], trio_mine[1], trio_mine[2], vectors], 1)
        other = jnp.concatenate([trio_other[0], trio_other[1], trio_other[2], vectors], 1)
        cols = by_core(core, mine, links.core_swap(other), 0)
        small = jnp.concatenate(
            [
                cols[:, split : split + 8],
                ffn_bias.reshape(chip_rows, 2),
                jnp.zeros((chip_rows, SMALL - 10), BF),
            ],
            1,
        )
        attn_block = jnp.concatenate([cols[:, :split], small], 1)
        attn = Flow(links.gather(attn_block, True, ((0, split), (split, split + SMALL))))
        down = Flow(links.gather(ffn_out, False))
        (got_tokens,) = release(attn, down, ties=(got_tokens,))
        tokens = jnp.concatenate([keep, got_tokens], 0)
        release(attn, down)
        release(attn)
        release(down)

        ffn_cols = ffn_in.reshape(own_rows, chips, 2, hidden).transpose(0, 2, 1, 3)
        ffn_cols = ffn_cols.reshape(own_rows, 2, chips * hidden)
        out_mine, out_other = halves(out_proj)
        mine = jnp.concatenate([pick(ffn_cols, core, 1), out_mine], 1)
        other = jnp.concatenate([pick(ffn_cols, 1 - core, 1), out_other], 1)
        cols = by_core(core, mine, links.core_swap(other), 0)
        up = Flow(links.gather(cols, True, ((0, FF // 2), (FF // 2, FF // 2 + HALF))))
        all_tokens = jnp.concatenate([tokens, links.core_swap(tokens)], 0)
        release(attn, up)
        (all_tokens,) = release(attn, up, ties=(all_tokens,))
        (all_tokens,) = release(up, ties=(all_tokens,))
        attn_pack = finish(attn)
        trio_weight = attn_pack[0].reshape(D, split)
        small = attn_pack[1]
        bias = small[..., :8].reshape(D, 8).T.astype(F32)
        up_bias = small[..., 8:10].reshape(FF // 2).astype(F32)

        slot_ids = pick(doc_ids, side, 0).reshape(2, 2, shard)
        slot_ids = jnp.stack(
            [
                slot_ids[side, core],
                slot_ids[1 - side, core],
                slot_ids[side, 1 - core],
                slot_ids[1 - side, 1 - core],
            ]
        )
        id_col = slot_ids.reshape(-1, 1)
        id_row = slot_ids.reshape(1, -1)
        low, high = jnp.min(slot_ids, 1), jnp.max(slot_ids, 1)

        own_bias = pick(bias[:2].reshape(2, 2, HALF), core, 1)
        zero = jnp.zeros_like(own_bias[0])
        trio_bias = jnp.concatenate([own_bias[0], zero, own_bias[1]])
        trio_scale = jnp.concatenate([zero + 0.125, zero + 1.0, zero + 1.0])
        trios = ((matmul(all_tokens, trio_weight) + trio_bias) * trio_scale).astype(BF)
        trios, row_grads = release(up, down, ties=(trios, out_grad))
        got_grads = links.row_swap(pick(row_grads, 1 - side, 0))
        mixed_heads, lse = attend(trios, low, high, id_col, id_row)
        mixed_heads, got_grads = release(up, down, ties=(mixed_heads, got_grads))
        grad_out = jnp.concatenate([pick(row_grads, side, 0), got_grads], 0).astype(F32)
        up_weight, out_half = finish(up)
        down_weight = finish(down)[0][0]
        up_weight = up_weight.reshape(D, FF // 2)
        out_half = out_half.reshape(D, HALF)
        out_weight = by_core(core, out_half, links.core_swap(out_half), 1)
        count = tokens.shape[0]
        mixed = by_core(core, mixed_heads[:count], links.core_swap(mixed_heads[count:]), 1)

        first_sum = tokens.astype(F32) + matmul(mixed, out_weight) + bias[2]
        first_normal, first_scale = normalize(first_sum)
        normed = first_normal * bias[6] + bias[3]
        normed_low = normed.astype(BF)
        all_normed = lax.optimization_barrier(
            jnp.concatenate([normed_low, links.core_swap(normed_low)], 0)
        )
        upper = matmul(all_normed, up_weight) + up_bias
        erf_part = 1.0 + lax.erf(upper * 0.7071067811865476)
        active = (0.5 * upper * erf_part).astype(BF)
        slope = 0.5 * erf_part + upper * jnp.exp(-0.5 * upper * upper) * 0.3989422804014327
        active, slope = lax.optimization_barrier((active, slope))
        partial = matmul(active, down_weight)
        second_sum = (
            normed
            + partial[:count]
            + links.core_swap(partial[count:].astype(BF)).astype(F32)
            + bias[4]
        )
        second_normal, second_scale = normalize(second_sum)
        result = (second_normal * bias[7] + bias[5]).astype(BF)

        def home(rows, got):
            kept = rows[:shard]
            return jnp.where(side == 0, jnp.stack([kept, got]), jnp.stack([got, kept]))

        got_result = links.row_swap(result[shard:])

        grad_second = normalize_back(grad_out * bias[7], second_normal, second_scale)
        grad_down = grad_second.astype(BF)
        all_down = lax.optimization_barrier(
            jnp.concatenate([grad_down, links.core_swap(grad_down)], 0)
        )
        grad_upper, partial, partial_other = hidden_back(all_down, down_weight, slope, up_weight)
        down_sum = Flow(links.scatter(active, all_down))
        (partial_got,) = release(down_sum, ties=(links.core_swap(partial_other),))
        grad_normed = grad_second + partial + partial_got.astype(F32)
        (grad_upper,) = release(down_sum, ties=(grad_upper,))
        grad_first = normalize_back(grad_normed * bias[6], first_normal, first_scale)
        grad_attn = grad_first.astype(BF)
        grad_out_weight = left_inner(mixed, grad_attn).astype(BF)
        grad_mixed = times_transposed(grad_attn, out_weight).astype(BF)
        mine, other = halves(grad_mixed)
        grad_heads = jnp.concatenate([mine, links.core_swap(other)], 0)
        mine, other = halves(grad_out_weight)
        out_sum = (mine.astype(F32) + links.core_swap(other).astype(F32)).astype(BF)
        up_sum = Flow(links.scatter(all_normed, grad_upper, out_sum))
        (grad_heads,) = release(down_sum, up_sum, ties=(grad_heads,))
        (grad_heads,) = release(down_sum, ties=(grad_heads,))
        grad_trios, trio_sums = attend_back(
            trios, grad_heads, mixed_heads, low, high, id_col, id_row, lse
        )
        trio_sums = trio_sums[0].reshape(3, HALF)

        own_half = jnp.stack([trio_sums[0], trio_sums[2]])
        none = jnp.zeros_like(own_half)
        sums = jnp.concatenate(
            [
                by_core(core, own_half, none, 1),
                jnp.stack(
                    [
                        jnp.sum(grad_attn.astype(F32), 0),
                        jnp.sum(grad_normed, 0),
                        jnp.sum(grad_down.astype(F32), 0),
                        jnp.sum(grad_out, 0),
                        jnp.sum(grad_normed * first_normal, 0),
                        jnp.sum(grad_out * second_normal, 0),
                    ]
                ),
            ],
            0,
        )
        up_bias_sum = jnp.sum(grad_upper.astype(F32), 0).reshape(D, 2)
        small = jnp.concatenate(
            [sums.T, up_bias_sum, jnp.zeros((D, SMALL - 10), F32)], 1
        ).astype(BF)
        attn_sum = Flow(links.scatter(all_tokens, grad_trios, small))
        grad_trios, got_result = release(
            attn_sum, down_sum, up_sum, ties=(grad_trios, got_result)
        )
        layer_out = home(result, got_result)
        partial = times_transposed(grad_trios, trio_weight)
        grad_tokens = (
            grad_first
            + partial[:count]
            + links.core_swap(partial[count:].astype(BF)).astype(F32)
        )
        grad_tokens = grad_tokens.astype(BF)
        grad_in = home(grad_tokens, links.row_swap(grad_tokens[shard:]))

        release(attn_sum, down_sum, up_sum)
        release(up_sum)
        release(attn_sum)
        release(attn_sum)
        release(attn_sum, up_sum)
        down_total = finish(down_sum)[0]
        up_total = finish(up_sum)[0]
        attn_total = finish(attn_sum)[0]

        def both(array):
            rows = array.reshape(2, own_rows, -1)
            other = links.core_swap(pick(rows, 1 - core, 0).astype(BF))
            return pick(rows, core, 0), other.astype(F32)

        mine, got = both(up_total)
        grad_ffn_in = by_core(
            core,
            mine[:, : FF // 2].reshape(own_rows, chips, 1, hidden),
            got[:, : FF // 2].reshape(own_rows, chips, 1, hidden),
            2,
        ).reshape(own_rows, FF)
        grad_out_proj = by_core(core, mine[:, FF // 2 :], got[:, FF // 2 :], 1)
        mine, got = both(attn_total)
        grad_in_proj = jnp.stack(
            [
                by_core(core, mine[:, i * HALF : (i + 1) * HALF], got[:, i * HALF : (i + 1) * HALF], 1)
                for i in range(3)
            ]
        )
        vectors = (mine[:, split : split + 8] + got[:, split : split + 8]).T
        grad_ffn_bias = attn_total[:, split + 8 : split + 10].reshape(hidden)
        return (
            layer_out,
            grad_in,
            grad_in_proj,
            grad_out_proj,
            vectors[:6],
            vectors[6:],
            grad_ffn_in,
            grad_ffn_bias,
            down_total,
        )

    return run


def solution(mesh):
    return jax.shard_map(
        local(mesh),
        mesh=mesh,
        in_specs=(
            P("wide", "narrow", None),
            P("wide", None),
            P(None, AXES, None),
            P(AXES, None),
            P(None, AXES),
            P(None, AXES),
            P(AXES, None),
            P(AXES),
            P(AXES, None),
            P("wide", "narrow", None),
        ),
        out_specs=(
            P("wide", "narrow", None),
            P("wide", "narrow", None),
            P(None, AXES, None),
            P(AXES, None),
            P(None, AXES),
            P(None, AXES),
            P(AXES, None),
            P(AXES),
            P(AXES, None),
        ),
        check_vma=False,
    )
```

```python
import functools

import jax
import jax.numpy as jnp
from jax import lax
from jax.experimental import pallas as pl
from jax.experimental.pallas import tpu as pltpu
from jax.sharding import PartitionSpec as P

D = 768
FF = 3072
DH = 64
PAIR = 128
HALF = D // 2
QB = 256
AXES = ("wide", "narrow")
EPS = 1e-05
BF = jnp.bfloat16
F32 = jnp.float32
MASKED = -1000000000.0
SMALL = 128
BRIEF = pl.CostEstimate(flops=1000, transcendentals=0, bytes_accessed=1000)


def matmul(left, right):
    return jnp.dot(left, right, preferred_element_type=F32)


def times_transposed(left, right):
    return lax.dot_general(left, right, (((1,), (1,)), ((), ())), preferred_element_type=F32)


def left_inner(left, right):
    return lax.dot_general(left, right, (((0,), (0,)), ((), ())), preferred_element_type=F32)


def overlap(low_ref, high_ref, key_block, query_block):
    return (low_ref[key_block] <= high_ref[query_block]) & (
        low_ref[query_block] <= high_ref[key_block]
    )


def tile_ids(id_col_ref, id_row_ref, keys, queries):
    return id_col_ref[keys, :] == id_row_ref[:, queries]


def one_head(rows, head):
    lane = lax.broadcasted_iota(jnp.int32, rows.shape, 1)
    return jnp.where((lane < DH) if head % 2 == 0 else (lane >= DH), rows, jnp.zeros_like(rows))


def attend_kernel(
    low_ref, high_ref, trio_ref, id_col_ref, id_row_ref, mixed_ref, lse_ref, vt_ref, acc_ref, top_ref, mass_ref
):
    total = trio_ref.shape[0]
    heads = HALF // DH
    blocks = total // QB
    vt_ref[...] = trio_ref[:, 2 * HALF :].T
    acc_ref[...] = jnp.zeros_like(acc_ref)
    mass_ref[...] = jnp.zeros_like(mass_ref)
    top_ref[...] = jnp.full_like(top_ref, -jnp.inf)

    def tile(step, carry):
        query_block, key_block = step // blocks, step % blocks

        @pl.when(overlap(low_ref, high_ref, key_block, query_block))
        def _():
            queries = pl.ds(pl.multiple_of(query_block * QB, QB), QB)
            keys = pl.ds(pl.multiple_of(key_block * QB, QB), QB)
            same = tile_ids(id_col_ref, id_row_ref, keys, queries)
            old_tops = top_ref[:, queries]
            old_mass = mass_ref[:, queries]

            def score(head):
                lanes = slice(head // 2 * PAIR, head // 2 * PAIR + PAIR)
                q = one_head(trio_ref[queries, lanes], head)
                k = trio_ref[keys, HALF + lanes.start : HALF + lanes.stop]
                return jnp.where(same, times_transposed(k, q), MASKED)

            scores = [score(head) for head in range(heads)]
            tops = [jnp.maximum(old_tops[h : h + 1], jnp.max(scores[h], 0, keepdims=True)) for h in range(heads)]
            weights = [jnp.exp(scores[h] - tops[h]) for h in range(heads)]
            shrinks = [jnp.exp(old_tops[h : h + 1] - tops[h]) for h in range(heads)]
            masses = [old_mass[h : h + 1] * shrinks[h] + jnp.sum(weights[h], 0, keepdims=True) for h in range(heads)]
            outs = [matmul(vt_ref[h * DH : (h + 1) * DH, keys], weights[h].astype(BF)) for h in range(heads)]
            for h in range(heads):
                rows = slice(h * DH, (h + 1) * DH)
                acc_ref[rows, queries] = acc_ref[rows, queries] * shrinks[h] + outs[h]
            top_ref[:, queries] = jnp.concatenate(tops + [old_tops[heads:]], 0)
            mass_ref[:, queries] = jnp.concatenate(masses + [old_mass[heads:]], 0)

        return carry

    lax.fori_loop(0, blocks * blocks, tile, 0)
    for head in range(heads):
        rows = slice(head * DH, (head + 1) * DH)
        acc_ref[rows, :] = acc_ref[rows, :] / mass_ref[head : head + 1, :]
    mixed_ref[...] = acc_ref[...].T.astype(BF)
    lse_ref[...] = top_ref[...] + jnp.log(mass_ref[...])


def attend(trios, low, high, id_col, id_row):
    total, width = trios.shape
    return pl.pallas_call(
        attend_kernel,
        grid_spec=pltpu.PrefetchScalarGridSpec(
            num_scalar_prefetch=2,
            grid=(1,),
            in_specs=[
                pl.BlockSpec((total, width), lambda p, *_: (0, 0)),
                pl.BlockSpec((total, 1), lambda p, *_: (0, 0)),
                pl.BlockSpec((1, total), lambda p, *_: (0, 0)),
            ],
            out_specs=[
                pl.BlockSpec((total, HALF), lambda p, *_: (0, 0)),
                pl.BlockSpec((8, total), lambda p, *_: (0, 0)),
            ],
            scratch_shapes=[
                pltpu.VMEM((HALF, total), BF),
                pltpu.VMEM((HALF, total), F32),
                pltpu.VMEM((8, total), F32),
                pltpu.VMEM((8, total), F32),
            ],
        ),
        out_shape=[
            jax.ShapeDtypeStruct((total, HALF), BF),
            jax.ShapeDtypeStruct((8, total), F32),
        ],
        cost_estimate=BRIEF,
        name="attend",
    )(low, high, trios, id_col, id_row)


def attend_back_kernel(
    low_ref,
    high_ref,
    trio_ref,
    grad_ref,
    mixed_ref,
    id_col_ref,
    id_row_ref,
    lse_ref,
    out_ref,
    sums_ref,
    kt_ref,
    inner_ref,
    dq_ref,
    dk_ref,
    dv_ref,
):
    total = trio_ref.shape[0]
    heads = HALF // DH
    blocks = total // QB
    kt_ref[...] = trio_ref[:, HALF : 2 * HALF].T
    dq_ref[...] = jnp.zeros_like(dq_ref)
    dk_ref[...] = jnp.zeros_like(dk_ref)
    dv_ref[...] = jnp.zeros_like(dv_ref)
    lane = lax.broadcasted_iota(jnp.int32, (8, HALF), 1)
    row = lax.broadcasted_iota(jnp.int32, (8, HALF), 0)
    chosen = jnp.where(lane // DH == row, 1.0, 0.0)
    products = grad_ref[...].astype(F32) * mixed_ref[...].astype(F32)
    inner_ref[...] = lax.dot_general(
        chosen,
        products,
        (((1,), (1,)), ((), ())),
        precision=lax.Precision.HIGHEST,
        preferred_element_type=F32,
    )

    def tile(step, carry):
        query_block, key_block = step // blocks, step % blocks

        @pl.when(overlap(low_ref, high_ref, key_block, query_block))
        def _():
            queries = pl.ds(pl.multiple_of(query_block * QB, QB), QB)
            keys = pl.ds(pl.multiple_of(key_block * QB, QB), QB)
            same = tile_ids(id_col_ref, id_row_ref, keys, queries)
            tops = lse_ref[:, queries]
            inner = inner_ref[:, queries]
            q, k, v, g = [], [], [], []
            for head in range(heads):
                lanes = slice(head // 2 * PAIR, head // 2 * PAIR + PAIR)
                q.append(one_head(trio_ref[queries, lanes], head))
                g.append(one_head(grad_ref[queries, lanes], head))
                k.append(trio_ref[keys, HALF + lanes.start : HALF + lanes.stop])
                v.append(trio_ref[keys, 2 * HALF + lanes.start : 2 * HALF + lanes.stop])
            scores = [times_transposed(k[h], q[h]) for h in range(heads)]
            grad_probs = [times_transposed(v[h], g[h]) for h in range(heads)]
            probs = [jnp.where(same, jnp.exp(scores[h] - tops[h : h + 1]), 0.0) for h in range(heads)]
            grad_scores = [(probs[h] * (grad_probs[h] - inner[h : h + 1])).astype(BF) for h in range(heads)]
            probs = [probs[h].astype(BF) for h in range(heads)]
            dq = [matmul(kt_ref[h * DH : (h + 1) * DH, keys], grad_scores[h]) for h in range(heads)]
            dk = [matmul(grad_scores[h], q[h]) for h in range(heads)]
            dv = [matmul(probs[h], g[h]) for h in range(heads)]
            for h in range(heads):
                dq_ref[h * DH : (h + 1) * DH, queries] += dq[h]
            for pair in range(heads // 2):
                lanes = slice(pair * PAIR, pair * PAIR + PAIR)
                dk_ref[keys, lanes] += dk[2 * pair] + dk[2 * pair + 1]
                dv_ref[keys, lanes] += dv[2 * pair] + dv[2 * pair + 1]

        return carry

    lax.fori_loop(0, blocks * blocks, tile, 0)
    grads = (
        (dq_ref[...].T.astype(BF).astype(F32) * 0.125).astype(BF),
        dk_ref[...].astype(BF),
        dv_ref[...].astype(BF),
    )
    for part in range(3):
        lanes = slice(part * HALF, (part + 1) * HALF)
        out_ref[:, lanes] = grads[part]
        column = jnp.sum(grads[part].astype(F32), 0, keepdims=True)
        sums_ref[:, lanes] = jnp.broadcast_to(column, (8, HALF))


def attend_back(trios, grads, mixed, low, high, id_col, id_row, lse):
    total, width = trios.shape
    return pl.pallas_call(
        attend_back_kernel,
        grid_spec=pltpu.PrefetchScalarGridSpec(
            num_scalar_prefetch=2,
            grid=(1,),
            in_specs=[
                pl.BlockSpec((total, width), lambda p, *_: (0, 0)),
                pl.BlockSpec((total, HALF), lambda p, *_: (0, 0)),
                pl.BlockSpec((total, HALF), lambda p, *_: (0, 0)),
                pl.BlockSpec((total, 1), lambda p, *_: (0, 0)),
                pl.BlockSpec((1, total), lambda p, *_: (0, 0)),
                pl.BlockSpec((8, total), lambda p, *_: (0, 0)),
            ],
            out_specs=[
                pl.BlockSpec((total, width), lambda p, *_: (0, 0)),
                pl.BlockSpec((8, width), lambda p, *_: (0, 0)),
            ],
            scratch_shapes=[
                pltpu.VMEM((HALF, total), BF),
                pltpu.VMEM((8, total), F32),
                pltpu.VMEM((HALF, total), F32),
                pltpu.VMEM((total, HALF), F32),
                pltpu.VMEM((total, HALF), F32),
            ],
        ),
        out_shape=[
            jax.ShapeDtypeStruct((total, width), BF),
            jax.ShapeDtypeStruct((8, width), F32),
        ],
        cost_estimate=BRIEF,
        name="attend_back",
    )(low, high, trios, grads, mixed, id_col, id_row, lse)


def place_kernel(columns, index_ref, *refs):
    count = (len(refs) - 2 - len(columns)) // 2
    pieces, outs = refs[:count], refs[count : count + len(columns)]
    held = refs[count + len(columns) : -2]
    in_sem, out_sem = refs[-2:]
    arriving = [
        pltpu.make_async_copy(pieces[i], held[i], in_sem.at[i]) for i in range(count)
    ]
    for copy in arriving:
        copy.start()
    leaving = []
    for i in range(count):
        arriving[i].wait()
        for j, (start, stop) in enumerate(columns):
            copy = pltpu.make_async_copy(
                held[i].at[:, :, start:stop], outs[j].at[:, index_ref[i]], out_sem.at[i, j]
            )
            copy.start()
            leaving.append(copy)
    for copy in leaving:
        copy.wait()


def place(pieces, index, columns):
    count = len(pieces)
    outer, rows, _ = pieces[0].shape
    anywhere = pl.BlockSpec(memory_space=pl.ANY)
    return pl.pallas_call(
        functools.partial(place_kernel, columns),
        grid_spec=pltpu.PrefetchScalarGridSpec(
            num_scalar_prefetch=1,
            grid=(1,),
            in_specs=[anywhere] * count,
            out_specs=[anywhere] * len(columns),
            scratch_shapes=[pltpu.VMEM(piece.shape, piece.dtype) for piece in pieces]
            + [pltpu.SemaphoreType.DMA((count,)), pltpu.SemaphoreType.DMA((count, len(columns)))],
        ),
        out_shape=[
            jax.ShapeDtypeStruct((outer, count, rows, stop - start), pieces[0].dtype)
            for start, stop in columns
        ],
        cost_estimate=BRIEF,
        name="place",
    )(index, *pieces)


def take_kernel(columns, count, index_ref, *refs):
    arrays = refs[: len(columns)]
    outs = refs[len(columns) : len(columns) + count]
    held = refs[len(columns) + count : -2]
    in_sem, out_sem = refs[-2:]
    arriving = []
    for i in range(count):
        for j, (start, stop) in enumerate(columns):
            copy = pltpu.make_async_copy(
                arrays[j].at[:, index_ref[i]], held[i].at[:, :, start:stop], in_sem.at[i, j]
            )
            copy.start()
            arriving.append(copy)
    leaving = []
    for i in range(count):
        for copy in arriving[i * len(columns) : (i + 1) * len(columns)]:
            copy.wait()
        copy = pltpu.make_async_copy(held[i], outs[i], out_sem.at[i])
        copy.start()
        leaving.append(copy)
    for copy in leaving:
        copy.wait()


def take(arrays, index):
    outer, count, rows, _ = arrays[0].shape
    columns, start = [], 0
    for array in arrays:
        columns.append((start, start + array.shape[3]))
        start += array.shape[3]
    anywhere = pl.BlockSpec(memory_space=pl.ANY)
    return pl.pallas_call(
        functools.partial(take_kernel, tuple(columns), count),
        grid_spec=pltpu.PrefetchScalarGridSpec(
            num_scalar_prefetch=1,
            grid=(1,),
            in_specs=[anywhere] * len(arrays),
            out_specs=[anywhere] * count,
            scratch_shapes=[pltpu.VMEM((outer, rows, start), BF) for _ in range(count)]
            + [pltpu.SemaphoreType.DMA((count, len(arrays))), pltpu.SemaphoreType.DMA((count,))],
        ),
        out_shape=[jax.ShapeDtypeStruct((outer, rows, start), BF)] * count,
        cost_estimate=BRIEF,
        name="take",
    )(index, *arrays)


def weight_grad_kernel(outer, count, rows, index_ref, left_ref, right_ref, *refs):
    extra_ref = refs[0] if len(refs) > count + 1 else None
    outs, held_ref = refs[-1 - count : -1], refs[-1]
    width = right_ref.shape[1]
    held_ref[...] = left_inner(left_ref[...], right_ref[...]).astype(BF)
    for i in range(count):
        for part in range(outer):
            source = pl.ds(pl.multiple_of((part * count + index_ref[i]) * rows, 16), rows)
            outs[i][part, :, :width] = held_ref[source, :]
            if extra_ref is not None:
                outs[i][part, :, width:] = extra_ref[source, :]


def weight_grad(left, right, extra, index, count, rows):
    outer = left.shape[1] // (count * rows)
    arrays = [left, right] + ([] if extra is None else [extra])
    if rows % 16:
        wide = left_inner(left, right).astype(BF)
        wide = wide if extra is None else jnp.concatenate([wide, extra], 1)
        return take([wide.reshape(outer, count, rows, -1)], index)
    width = sum(array.shape[1] for array in arrays[1:])
    return pl.pallas_call(
        functools.partial(weight_grad_kernel, outer, count, rows),
        grid_spec=pltpu.PrefetchScalarGridSpec(
            num_scalar_prefetch=1,
            grid=(1,),
            in_specs=[pl.BlockSpec(array.shape, lambda p, *_: (0, 0)) for array in arrays],
            out_specs=[pl.BlockSpec((outer, rows, width), lambda p, *_: (0, 0, 0))] * count,
            scratch_shapes=[pltpu.VMEM((left.shape[1], right.shape[1]), BF)],
        ),
        out_shape=[jax.ShapeDtypeStruct((outer, rows, width), BF)] * count,
        cost_estimate=BRIEF,
        name="weight_grad",
    )(index, *arrays)


def hidden_back_kernel(own_steps, rows_ref, down_ref, slope_ref, up_ref, grad_ref, own_ref, other_ref):
    grad = (times_transposed(rows_ref[...], down_ref[...]) * slope_ref[...]).astype(BF)
    grad_ref[...] = grad
    partial = times_transposed(grad, up_ref[...])

    @pl.when(pl.program_id(0) < own_steps)
    def _():
        own_ref[...] = partial

    @pl.when(pl.program_id(0) >= own_steps)
    def _():
        other_ref[...] = partial.astype(BF)


def hidden_back(rows, down, slope, up):
    total, width = rows.shape
    units = slope.shape[1]
    block = 256 if total % 512 == 0 else total // 2
    own_steps = total // 2 // block
    return pl.pallas_call(
        functools.partial(hidden_back_kernel, own_steps),
        grid=(total // block,),
        in_specs=[
            pl.BlockSpec((block, width), lambda i: (i, 0)),
            pl.BlockSpec((units, width), lambda i: (0, 0), pipeline_mode=pl.Buffered(1)),
            pl.BlockSpec((block, units), lambda i: (i, 0)),
            pl.BlockSpec((width, units), lambda i: (0, 0), pipeline_mode=pl.Buffered(1)),
        ],
        out_specs=[
            pl.BlockSpec((block, units), lambda i: (i, 0)),
            pl.BlockSpec((block, width), lambda i: (jnp.minimum(i, own_steps - 1), 0)),
            pl.BlockSpec((block, width), lambda i: (jnp.maximum(i - own_steps, 0), 0)),
        ],
        out_shape=[
            jax.ShapeDtypeStruct((total, units), BF),
            jax.ShapeDtypeStruct((total // 2, width), F32),
            jax.ShapeDtypeStruct((total // 2, width), BF),
        ],
        cost_estimate=BRIEF,
        name="hidden_back",
    )(rows, down, slope, up)


def sum_take_kernel(count, index_ref, *refs):
    arrays, outs = refs[:-count], refs[-count:]
    for i in range(count):
        total = arrays[0][:, index_ref[i]].astype(F32)
        for array in arrays[1:]:
            total += array[:, index_ref[i]].astype(F32)
        outs[i][...] = total.astype(BF)


def sum_take(arrays, index, count):
    arrays = [array.reshape((-1, count) + array.shape[1:]) for array in arrays]
    outer, _, rows, width = arrays[0].shape
    return pl.pallas_call(
        functools.partial(sum_take_kernel, count),
        grid_spec=pltpu.PrefetchScalarGridSpec(
            num_scalar_prefetch=1,
            grid=(1,),
            in_specs=[pl.BlockSpec(array.shape, lambda p, *_: (0, 0, 0, 0)) for array in arrays],
            out_specs=[pl.BlockSpec((outer, rows, width), lambda p, *_: (0, 0, 0))] * count,
        ),
        out_shape=[jax.ShapeDtypeStruct((outer, rows, width), BF)] * count,
        cost_estimate=BRIEF,
        name="sum_take",
    )(index, *arrays)


class Links:
    def __init__(self, mesh):
        self.devices = mesh.shape["wide"] * mesh.shape["narrow"]
        self.chips = self.devices // 2
        bits = self.chips.bit_length() - 1
        assert self.chips == 1 << bits
        self.groups = [(low, 2) for low in range(bits - 2, -1, -2)]
        if bits % 2:
            self.groups.append((0, 1))
        self.own = lax.axis_index(AXES)
        self.chip = self.own // 2
        self.core = self.own % 2

    def send(self, value, flip_even, flip_odd):
        pairs = [(d, d ^ (flip_odd if d % 2 else flip_even)) for d in range(self.devices)]
        return lax.ppermute(value, AXES, pairs)

    def core_swap(self, value):
        return self.send(value, 1, 1)

    def row_swap(self, value):
        return self.send(value, 2, 2)

    def spots(self, low, size):
        place = (self.chip >> low) % (1 << size)
        if size == 1:
            return jnp.stack([place, place ^ 1]).astype(jnp.int32)
        first, second = 1 + self.core, 2 - self.core
        return jnp.stack([place, place ^ first, place ^ second, place ^ 3]).astype(jnp.int32)

    def gather(self, block, high, columns=None):
        width = block.shape[1]
        have = block[None]
        groups = self.groups if high else self.groups[::-1]
        for stage, (low, size) in enumerate(groups):
            if size == 1:
                (one,) = yield (self.send(have, 2 << low, 2 << low),)
                yield ()
                pieces = [have, one]
            else:
                one = self.send(have, 2 << low, 4 << low)
                two = self.send(have, 4 << low, 2 << low)
                one, two = yield (one, two)
                (three,) = yield (self.send(one, 4 << low, 2 << low),)
                pieces = [have, one, two, three]
            last = stage == len(groups) - 1
            placed = place(pieces, self.spots(low, size), columns if last and columns else ((0, width),))
            if high:
                placed = [out.reshape((-1,) + out.shape[2:]) for out in placed]
            else:
                placed = [out.reshape(1, -1, out.shape[3]) for out in placed]
            placed = yield tuple(placed)
            have = placed[0]

    def scatter(self, left, right, extra=None):
        rows = left.shape[1] // self.chips
        for stage, (low, size) in enumerate(self.groups[::-1]):
            spots, count = self.spots(low, size), 1 << size
            if stage:
                pieces = sum_take(parts, spots, count)
            else:
                pieces = weight_grad(left, right, extra, spots, count, rows)
            pieces = yield tuple(pieces)
            if size == 1:
                (got,) = yield (self.send(pieces[1], 2 << low, 2 << low),)
                yield ()
                parts = [pieces[0], got]
            else:
                three = self.send(pieces[3], 4 << low, 2 << low)
                two = self.send(pieces[2], 4 << low, 2 << low)
                three, two = yield (three, two)
                one = (pieces[1].astype(F32) + three.astype(F32)).astype(BF)
                (one,) = yield (self.send(one, 2 << low, 4 << low),)
                parts = [pieces[0], two, one]
        yield (sum(part[0].astype(F32) for part in parts),)


class Flow:
    def __init__(self, steps):
        self.steps = steps
        self.pending = next(steps)
        self.running = True

    def go(self, values):
        try:
            self.pending = self.steps.send(values)
        except StopIteration:
            self.pending = values
            self.running = False


def release(*flows, ties=()):
    held = lax.optimization_barrier((tuple(flow.pending for flow in flows), ties))
    for flow, values in zip(flows, held[0]):
        flow.go(values)
    return held[1]


def finish(flow):
    while flow.running:
        release(flow)
    return flow.pending


def after(value, others):
    return lax.optimization_barrier((value, others))[0]


def pick(parts, at, axis):
    return lax.dynamic_index_in_dim(parts, at, axis, keepdims=False)


def by_core(core, own, other, axis):
    return jnp.where(
        core == 0, jnp.concatenate([own, other], axis), jnp.concatenate([other, own], axis)
    )


def normalize(rows):
    average = jnp.mean(rows, -1, keepdims=True)
    centered = rows - average
    scale = lax.rsqrt(jnp.mean(centered * centered, -1, keepdims=True) + EPS)
    return centered * scale, scale


def normalize_back(grads, normal, scale):
    return (
        grads
        - jnp.mean(grads, -1, keepdims=True)
        - normal * jnp.mean(grads * normal, -1, keepdims=True)
    ) * scale


def local(mesh):
    def run(
        layer_in, doc_ids, in_proj, out_proj, vec_bias, norm_gain, ffn_in, ffn_bias, ffn_out, out_grad
    ):
        links = Links(mesh)
        core, chips = links.core, links.chips
        side = (links.own // 2) % 2
        slots, shard, _ = layer_in.shape
        assert slots == 2 and mesh.shape["narrow"] == 4
        own_rows = in_proj.shape[1]
        chip_rows = 2 * own_rows
        hidden = ffn_out.shape[0]

        def halves(array):
            left, right = jnp.split(array, 2, -1)
            return jnp.where(core == 0, left, right), jnp.where(core == 0, right, left)

        keep = pick(layer_in, side, 0)
        got_tokens = links.row_swap(pick(layer_in, 1 - side, 0))

        split = 3 * HALF
        trio_mine, trio_other = halves(in_proj)
        vectors = jnp.pad(jnp.concatenate([vec_bias, norm_gain], 0).T, ((0, 0), (0, SMALL - 8)))
        mine = jnp.concatenate([trio_mine[0], trio_mine[1], trio_mine[2], vectors], 1)
        other = jnp.concatenate([trio_other[0], trio_other[1], trio_other[2], vectors], 1)
        cols = by_core(core, mine, links.core_swap(other), 0)
        small = jnp.concatenate(
            [
                cols[:, split : split + 8],
                ffn_bias.reshape(chip_rows, 2),
                jnp.zeros((chip_rows, SMALL - 10), BF),
            ],
            1,
        )
        attn_block = jnp.concatenate([cols[:, :split], small], 1)
        attn = Flow(links.gather(attn_block, True, ((0, split), (split, split + SMALL))))
        down = Flow(links.gather(ffn_out, False))
        (got_tokens,) = release(attn, down, ties=(got_tokens,))
        tokens = jnp.concatenate([keep, got_tokens], 0)
        release(attn, down)
        release(attn)
        release(down)

        ffn_cols = ffn_in.reshape(own_rows, chips, 2, hidden).transpose(0, 2, 1, 3)
        ffn_cols = ffn_cols.reshape(own_rows, 2, chips * hidden)
        out_mine, out_other = halves(out_proj)
        mine = jnp.concatenate([pick(ffn_cols, core, 1), out_mine], 1)
        other = jnp.concatenate([pick(ffn_cols, 1 - core, 1), out_other], 1)
        cols = by_core(core, mine, links.core_swap(other), 0)
        up = Flow(links.gather(cols, True, ((0, FF // 2), (FF // 2, FF // 2 + HALF))))
        all_tokens = jnp.concatenate([tokens, links.core_swap(tokens)], 0)
        release(attn, up)
        (all_tokens,) = release(attn, up, ties=(all_tokens,))
        (all_tokens,) = release(up, ties=(all_tokens,))
        attn_pack = finish(attn)
        trio_weight = attn_pack[0].reshape(D, split)
        small = attn_pack[1]
        bias = small[..., :8].reshape(D, 8).T.astype(F32)
        up_bias = small[..., 8:10].reshape(FF // 2).astype(F32)

        slot_ids = pick(doc_ids, side, 0).reshape(2, 2, shard)
        slot_ids = jnp.stack(
            [
                slot_ids[side, core],
                slot_ids[1 - side, core],
                slot_ids[side, 1 - core],
                slot_ids[1 - side, 1 - core],
            ]
        )
        id_col = slot_ids.reshape(-1, 1)
        id_row = slot_ids.reshape(1, -1)
        low, high = jnp.min(slot_ids, 1), jnp.max(slot_ids, 1)

        own_bias = pick(bias[:2].reshape(2, 2, HALF), core, 1)
        zero = jnp.zeros_like(own_bias[0])
        trio_bias = jnp.concatenate([own_bias[0], zero, own_bias[1]])
        trio_scale = jnp.concatenate([zero + 0.125, zero + 1.0, zero + 1.0])
        trios = ((matmul(all_tokens, trio_weight) + trio_bias) * trio_scale).astype(BF)
        trios, row_grads = release(up, down, ties=(trios, out_grad))
        got_grads = links.row_swap(pick(row_grads, 1 - side, 0))
        mixed_heads, lse = attend(trios, low, high, id_col, id_row)
        mixed_heads, got_grads = release(up, down, ties=(mixed_heads, got_grads))
        grad_out = jnp.concatenate([pick(row_grads, side, 0), got_grads], 0).astype(F32)
        up_weight, out_half = finish(up)
        down_weight = finish(down)[0][0]
        up_weight = up_weight.reshape(D, FF // 2)
        out_half = out_half.reshape(D, HALF)
        out_weight = by_core(core, out_half, links.core_swap(out_half), 1)
        count = tokens.shape[0]
        mixed = by_core(core, mixed_heads[:count], links.core_swap(mixed_heads[count:]), 1)

        first_sum = tokens.astype(F32) + matmul(mixed, out_weight) + bias[2]
        first_normal, first_scale = normalize(first_sum)
        normed = first_normal * bias[6] + bias[3]
        normed_low = normed.astype(BF)
        all_normed = lax.optimization_barrier(
            jnp.concatenate([normed_low, links.core_swap(normed_low)], 0)
        )
        upper = matmul(all_normed, up_weight) + up_bias
        erf_part = 1.0 + lax.erf(upper * 0.7071067811865476)
        active = (0.5 * upper * erf_part).astype(BF)
        slope = 0.5 * erf_part + upper * jnp.exp(-0.5 * upper * upper) * 0.3989422804014327
        active, slope = lax.optimization_barrier((active, slope))
        partial = matmul(active, down_weight)
        second_sum = (
            normed
            + partial[:count]
            + links.core_swap(partial[count:].astype(BF)).astype(F32)
            + bias[4]
        )
        second_normal, second_scale = normalize(second_sum)
        result = (second_normal * bias[7] + bias[5]).astype(BF)

        def home(rows, got):
            kept = rows[:shard]
            return jnp.where(side == 0, jnp.stack([kept, got]), jnp.stack([got, kept]))

        got_result = links.row_swap(result[shard:])

        grad_second = normalize_back(grad_out * bias[7], second_normal, second_scale)
        grad_down = grad_second.astype(BF)
        all_down = lax.optimization_barrier(
            jnp.concatenate([grad_down, links.core_swap(grad_down)], 0)
        )
        grad_upper, partial, partial_other = hidden_back(all_down, down_weight, slope, up_weight)
        down_sum = Flow(links.scatter(active, all_down))
        (partial_got,) = release(down_sum, ties=(links.core_swap(partial_other),))
        grad_normed = grad_second + partial + partial_got.astype(F32)
        grad_first = normalize_back(grad_normed * bias[6], first_normal, first_scale)
        grad_attn = grad_first.astype(BF)
        grad_out_weight = left_inner(mixed, grad_attn).astype(BF)
        grad_mixed = times_transposed(grad_attn, out_weight).astype(BF)
        mine, other = halves(grad_mixed)
        grad_heads = jnp.concatenate([mine, links.core_swap(other)], 0)
        mine, other = halves(grad_out_weight)
        out_sum = (mine.astype(F32) + links.core_swap(other).astype(F32)).astype(BF)
        up_sum = Flow(links.scatter(all_normed, grad_upper, out_sum))
        (grad_heads,) = release(down_sum, up_sum, ties=(grad_heads,))
        grad_trios, trio_sums = attend_back(
            trios, grad_heads, mixed_heads, low, high, id_col, id_row, lse
        )
        trio_sums = trio_sums[0].reshape(3, HALF)

        own_half = jnp.stack([trio_sums[0], trio_sums[2]])
        none = jnp.zeros_like(own_half)
        sums = jnp.concatenate(
            [
                by_core(core, own_half, none, 1),
                jnp.stack(
                    [
                        jnp.sum(grad_attn.astype(F32), 0),
                        jnp.sum(grad_normed, 0),
                        jnp.sum(grad_down.astype(F32), 0),
                        jnp.sum(grad_out, 0),
                        jnp.sum(grad_normed * first_normal, 0),
                        jnp.sum(grad_out * second_normal, 0),
                    ]
                ),
            ],
            0,
        )
        up_bias_sum = jnp.sum(grad_upper.astype(F32), 0).reshape(D, 2)
        small = jnp.concatenate(
            [sums.T, up_bias_sum, jnp.zeros((D, SMALL - 10), F32)], 1
        ).astype(BF)
        attn_sum = Flow(links.scatter(all_tokens, grad_trios, small))
        grad_trios, got_result = release(
            attn_sum, down_sum, up_sum, ties=(grad_trios, got_result)
        )
        layer_out = home(result, got_result)
        partial = times_transposed(grad_trios, trio_weight)
        grad_tokens = (
            grad_first
            + partial[:count]
            + links.core_swap(partial[count:].astype(BF)).astype(F32)
        )
        grad_tokens = grad_tokens.astype(BF)
        grad_in = home(grad_tokens, links.row_swap(grad_tokens[shard:]))

        release(up_sum, down_sum)
        release(attn_sum, up_sum)
        release(attn_sum, up_sum)
        release(attn_sum)
        release(attn_sum, up_sum, down_sum)
        down_total = finish(down_sum)[0]
        up_total = finish(up_sum)[0]
        attn_total = finish(attn_sum)[0]

        def both(array):
            rows = array.reshape(2, own_rows, -1)
            other = links.core_swap(pick(rows, 1 - core, 0).astype(BF))
            return pick(rows, core, 0), other.astype(F32)

        mine, got = both(up_total)
        grad_ffn_in = by_core(
            core,
            mine[:, : FF // 2].reshape(own_rows, chips, 1, hidden),
            got[:, : FF // 2].reshape(own_rows, chips, 1, hidden),
            2,
        ).reshape(own_rows, FF)
        grad_out_proj = by_core(core, mine[:, FF // 2 :], got[:, FF // 2 :], 1)
        mine, got = both(attn_total)
        grad_in_proj = jnp.stack(
            [
                by_core(core, mine[:, i * HALF : (i + 1) * HALF], got[:, i * HALF : (i + 1) * HALF], 1)
                for i in range(3)
            ]
        )
        vectors = (mine[:, split : split + 8] + got[:, split : split + 8]).T
        grad_ffn_bias = attn_total[:, split + 8 : split + 10].reshape(hidden)
        return (
            layer_out,
            grad_in,
            grad_in_proj,
            grad_out_proj,
            vectors[:6],
            vectors[6:],
            grad_ffn_in,
            grad_ffn_bias,
            down_total,
        )

    return run


def solution(mesh):
    return jax.shard_map(
        local(mesh),
        mesh=mesh,
        in_specs=(
            P("wide", "narrow", None),
            P("wide", None),
            P(None, AXES, None),
            P(AXES, None),
            P(None, AXES),
            P(None, AXES),
            P(AXES, None),
            P(AXES),
            P(AXES, None),
            P("wide", "narrow", None),
        ),
        out_specs=(
            P("wide", "narrow", None),
            P("wide", "narrow", None),
            P(None, AXES, None),
            P(AXES, None),
            P(None, AXES),
            P(None, AXES),
            P(AXES, None),
            P(AXES),
            P(AXES, None),
        ),
        check_vma=False,
    )
```

```python
import functools

import jax
import jax.numpy as jnp
from jax import lax
from jax.experimental import pallas as pl
from jax.experimental.pallas import tpu as pltpu
from jax.sharding import PartitionSpec as P

D = 768
FF = 3072
DH = 64
PAIR = 128
HALF = D // 2
QB = 256
AXES = ("wide", "narrow")
EPS = 1e-05
BF = jnp.bfloat16
F32 = jnp.float32
MASKED = -1000000000.0
SMALL = 128
BRIEF = pl.CostEstimate(flops=1000, transcendentals=0, bytes_accessed=1000)


def matmul(left, right):
    return jnp.dot(left, right, preferred_element_type=F32)


def times_transposed(left, right):
    return lax.dot_general(left, right, (((1,), (1,)), ((), ())), preferred_element_type=F32)


def left_inner(left, right):
    return lax.dot_general(left, right, (((0,), (0,)), ((), ())), preferred_element_type=F32)


def overlap(low_ref, high_ref, key_block, query_block):
    return (low_ref[key_block] <= high_ref[query_block]) & (
        low_ref[query_block] <= high_ref[key_block]
    )


def tile_ids(id_col_ref, id_row_ref, keys, queries):
    return id_col_ref[keys, :] == id_row_ref[:, queries]


def one_head(rows, head):
    lane = lax.broadcasted_iota(jnp.int32, rows.shape, 1)
    return jnp.where((lane < DH) if head % 2 == 0 else (lane >= DH), rows, jnp.zeros_like(rows))


def attend_kernel(
    low_ref, high_ref, trio_ref, id_col_ref, id_row_ref, mixed_ref, lse_ref, vt_ref, acc_ref, top_ref, mass_ref
):
    total = trio_ref.shape[0]
    heads = HALF // DH
    blocks = total // QB
    vt_ref[...] = trio_ref[:, 2 * HALF :].T
    acc_ref[...] = jnp.zeros_like(acc_ref)
    mass_ref[...] = jnp.zeros_like(mass_ref)
    top_ref[...] = jnp.full_like(top_ref, -jnp.inf)

    def tile(step, carry):
        query_block, key_block = step // blocks, step % blocks

        @pl.when(overlap(low_ref, high_ref, key_block, query_block))
        def _():
            queries = pl.ds(pl.multiple_of(query_block * QB, QB), QB)
            keys = pl.ds(pl.multiple_of(key_block * QB, QB), QB)
            same = tile_ids(id_col_ref, id_row_ref, keys, queries)
            old_tops = top_ref[:, queries]
            old_mass = mass_ref[:, queries]

            def score(head):
                lanes = slice(head // 2 * PAIR, head // 2 * PAIR + PAIR)
                q = one_head(trio_ref[queries, lanes], head)
                k = trio_ref[keys, HALF + lanes.start : HALF + lanes.stop]
                return jnp.where(same, times_transposed(k, q), MASKED)

            scores = [score(head) for head in range(heads)]
            tops = [jnp.maximum(old_tops[h : h + 1], jnp.max(scores[h], 0, keepdims=True)) for h in range(heads)]
            weights = [jnp.exp(scores[h] - tops[h]) for h in range(heads)]
            shrinks = [jnp.exp(old_tops[h : h + 1] - tops[h]) for h in range(heads)]
            masses = [old_mass[h : h + 1] * shrinks[h] + jnp.sum(weights[h], 0, keepdims=True) for h in range(heads)]
            outs = [matmul(vt_ref[h * DH : (h + 1) * DH, keys], weights[h].astype(BF)) for h in range(heads)]
            for h in range(heads):
                rows = slice(h * DH, (h + 1) * DH)
                acc_ref[rows, queries] = acc_ref[rows, queries] * shrinks[h] + outs[h]
            top_ref[:, queries] = jnp.concatenate(tops + [old_tops[heads:]], 0)
            mass_ref[:, queries] = jnp.concatenate(masses + [old_mass[heads:]], 0)

        return carry

    lax.fori_loop(0, blocks * blocks, tile, 0)
    for head in range(heads):
        rows = slice(head * DH, (head + 1) * DH)
        acc_ref[rows, :] = acc_ref[rows, :] / mass_ref[head : head + 1, :]
    mixed_ref[...] = acc_ref[...].T.astype(BF)
    lse_ref[...] = top_ref[...] + jnp.log(mass_ref[...])


def attend(trios, low, high, id_col, id_row):
    total, width = trios.shape
    return pl.pallas_call(
        attend_kernel,
        grid_spec=pltpu.PrefetchScalarGridSpec(
            num_scalar_prefetch=2,
            grid=(1,),
            in_specs=[
                pl.BlockSpec((total, width), lambda p, *_: (0, 0)),
                pl.BlockSpec((total, 1), lambda p, *_: (0, 0)),
                pl.BlockSpec((1, total), lambda p, *_: (0, 0)),
            ],
            out_specs=[
                pl.BlockSpec((total, HALF), lambda p, *_: (0, 0)),
                pl.BlockSpec((8, total), lambda p, *_: (0, 0)),
            ],
            scratch_shapes=[
                pltpu.VMEM((HALF, total), BF),
                pltpu.VMEM((HALF, total), F32),
                pltpu.VMEM((8, total), F32),
                pltpu.VMEM((8, total), F32),
            ],
        ),
        out_shape=[
            jax.ShapeDtypeStruct((total, HALF), BF),
            jax.ShapeDtypeStruct((8, total), F32),
        ],
        cost_estimate=BRIEF,
        name="attend",
    )(low, high, trios, id_col, id_row)


def attend_back_kernel(
    low_ref,
    high_ref,
    trio_ref,
    grad_ref,
    mixed_ref,
    id_col_ref,
    id_row_ref,
    lse_ref,
    out_ref,
    sums_ref,
    kt_ref,
    inner_ref,
    dq_ref,
    dk_ref,
    dv_ref,
):
    total = trio_ref.shape[0]
    heads = HALF // DH
    blocks = total // QB
    kt_ref[...] = trio_ref[:, HALF : 2 * HALF].T
    dq_ref[...] = jnp.zeros_like(dq_ref)
    dk_ref[...] = jnp.zeros_like(dk_ref)
    dv_ref[...] = jnp.zeros_like(dv_ref)
    lane = lax.broadcasted_iota(jnp.int32, (8, HALF), 1)
    row = lax.broadcasted_iota(jnp.int32, (8, HALF), 0)
    chosen = jnp.where(lane // DH == row, 1.0, 0.0)
    products = grad_ref[...].astype(F32) * mixed_ref[...].astype(F32)
    inner_ref[...] = lax.dot_general(
        chosen,
        products,
        (((1,), (1,)), ((), ())),
        precision=lax.Precision.HIGHEST,
        preferred_element_type=F32,
    )

    def tile(step, carry):
        query_block, key_block = step // blocks, step % blocks

        @pl.when(overlap(low_ref, high_ref, key_block, query_block))
        def _():
            queries = pl.ds(pl.multiple_of(query_block * QB, QB), QB)
            keys = pl.ds(pl.multiple_of(key_block * QB, QB), QB)
            same = tile_ids(id_col_ref, id_row_ref, keys, queries)
            tops = lse_ref[:, queries]
            inner = inner_ref[:, queries]
            q, k, v, g = [], [], [], []
            for head in range(heads):
                lanes = slice(head // 2 * PAIR, head // 2 * PAIR + PAIR)
                q.append(one_head(trio_ref[queries, lanes], head))
                g.append(one_head(grad_ref[queries, lanes], head))
                k.append(trio_ref[keys, HALF + lanes.start : HALF + lanes.stop])
                v.append(trio_ref[keys, 2 * HALF + lanes.start : 2 * HALF + lanes.stop])
            scores = [times_transposed(k[h], q[h]) for h in range(heads)]
            grad_probs = [times_transposed(v[h], g[h]) for h in range(heads)]
            probs = [jnp.where(same, jnp.exp(scores[h] - tops[h : h + 1]), 0.0) for h in range(heads)]
            grad_scores = [(probs[h] * (grad_probs[h] - inner[h : h + 1])).astype(BF) for h in range(heads)]
            probs = [probs[h].astype(BF) for h in range(heads)]
            dq = [matmul(kt_ref[h * DH : (h + 1) * DH, keys], grad_scores[h]) for h in range(heads)]
            dk = [matmul(grad_scores[h], q[h]) for h in range(heads)]
            dv = [matmul(probs[h], g[h]) for h in range(heads)]
            for h in range(heads):
                dq_ref[h * DH : (h + 1) * DH, queries] += dq[h]
            for pair in range(heads // 2):
                lanes = slice(pair * PAIR, pair * PAIR + PAIR)
                dk_ref[keys, lanes] += dk[2 * pair] + dk[2 * pair + 1]
                dv_ref[keys, lanes] += dv[2 * pair] + dv[2 * pair + 1]

        return carry

    lax.fori_loop(0, blocks * blocks, tile, 0)
    grads = (
        (dq_ref[...].T.astype(BF).astype(F32) * 0.125).astype(BF),
        dk_ref[...].astype(BF),
        dv_ref[...].astype(BF),
    )
    for part in range(3):
        lanes = slice(part * HALF, (part + 1) * HALF)
        out_ref[:, lanes] = grads[part]
        column = jnp.sum(grads[part].astype(F32), 0, keepdims=True)
        sums_ref[:, lanes] = jnp.broadcast_to(column, (8, HALF))


def attend_back(trios, grads, mixed, low, high, id_col, id_row, lse):
    total, width = trios.shape
    return pl.pallas_call(
        attend_back_kernel,
        grid_spec=pltpu.PrefetchScalarGridSpec(
            num_scalar_prefetch=2,
            grid=(1,),
            in_specs=[
                pl.BlockSpec((total, width), lambda p, *_: (0, 0)),
                pl.BlockSpec((total, HALF), lambda p, *_: (0, 0)),
                pl.BlockSpec((total, HALF), lambda p, *_: (0, 0)),
                pl.BlockSpec((total, 1), lambda p, *_: (0, 0)),
                pl.BlockSpec((1, total), lambda p, *_: (0, 0)),
                pl.BlockSpec((8, total), lambda p, *_: (0, 0)),
            ],
            out_specs=[
                pl.BlockSpec((total, width), lambda p, *_: (0, 0)),
                pl.BlockSpec((8, width), lambda p, *_: (0, 0)),
            ],
            scratch_shapes=[
                pltpu.VMEM((HALF, total), BF),
                pltpu.VMEM((8, total), F32),
                pltpu.VMEM((HALF, total), F32),
                pltpu.VMEM((total, HALF), F32),
                pltpu.VMEM((total, HALF), F32),
            ],
        ),
        out_shape=[
            jax.ShapeDtypeStruct((total, width), BF),
            jax.ShapeDtypeStruct((8, width), F32),
        ],
        cost_estimate=BRIEF,
        name="attend_back",
    )(low, high, trios, grads, mixed, id_col, id_row, lse)


def place_kernel(columns, index_ref, *refs):
    count = (len(refs) - 2 - len(columns)) // 2
    pieces, outs = refs[:count], refs[count : count + len(columns)]
    held = refs[count + len(columns) : -2]
    in_sem, out_sem = refs[-2:]
    arriving = [
        pltpu.make_async_copy(pieces[i], held[i], in_sem.at[i]) for i in range(count)
    ]
    for copy in arriving:
        copy.start()
    leaving = []
    for i in range(count):
        arriving[i].wait()
        for j, (start, stop) in enumerate(columns):
            copy = pltpu.make_async_copy(
                held[i].at[:, :, start:stop], outs[j].at[:, index_ref[i]], out_sem.at[i, j]
            )
            copy.start()
            leaving.append(copy)
    for copy in leaving:
        copy.wait()


def place(pieces, index, columns):
    count = len(pieces)
    outer, rows, _ = pieces[0].shape
    anywhere = pl.BlockSpec(memory_space=pl.ANY)
    return pl.pallas_call(
        functools.partial(place_kernel, columns),
        grid_spec=pltpu.PrefetchScalarGridSpec(
            num_scalar_prefetch=1,
            grid=(1,),
            in_specs=[anywhere] * count,
            out_specs=[anywhere] * len(columns),
            scratch_shapes=[pltpu.VMEM(piece.shape, piece.dtype) for piece in pieces]
            + [pltpu.SemaphoreType.DMA((count,)), pltpu.SemaphoreType.DMA((count, len(columns)))],
        ),
        out_shape=[
            jax.ShapeDtypeStruct((outer, count, rows, stop - start), pieces[0].dtype)
            for start, stop in columns
        ],
        cost_estimate=BRIEF,
        name="place",
    )(index, *pieces)


def take_kernel(columns, count, index_ref, *refs):
    arrays = refs[: len(columns)]
    outs = refs[len(columns) : len(columns) + count]
    held = refs[len(columns) + count : -2]
    in_sem, out_sem = refs[-2:]
    arriving = []
    for i in range(count):
        for j, (start, stop) in enumerate(columns):
            copy = pltpu.make_async_copy(
                arrays[j].at[:, index_ref[i]], held[i].at[:, :, start:stop], in_sem.at[i, j]
            )
            copy.start()
            arriving.append(copy)
    leaving = []
    for i in range(count):
        for copy in arriving[i * len(columns) : (i + 1) * len(columns)]:
            copy.wait()
        copy = pltpu.make_async_copy(held[i], outs[i], out_sem.at[i])
        copy.start()
        leaving.append(copy)
    for copy in leaving:
        copy.wait()


def take(arrays, index):
    outer, count, rows, _ = arrays[0].shape
    columns, start = [], 0
    for array in arrays:
        columns.append((start, start + array.shape[3]))
        start += array.shape[3]
    anywhere = pl.BlockSpec(memory_space=pl.ANY)
    return pl.pallas_call(
        functools.partial(take_kernel, tuple(columns), count),
        grid_spec=pltpu.PrefetchScalarGridSpec(
            num_scalar_prefetch=1,
            grid=(1,),
            in_specs=[anywhere] * len(arrays),
            out_specs=[anywhere] * count,
            scratch_shapes=[pltpu.VMEM((outer, rows, start), BF) for _ in range(count)]
            + [pltpu.SemaphoreType.DMA((count, len(arrays))), pltpu.SemaphoreType.DMA((count,))],
        ),
        out_shape=[jax.ShapeDtypeStruct((outer, rows, start), BF)] * count,
        cost_estimate=BRIEF,
        name="take",
    )(index, *arrays)


def weight_grad_kernel(outer, count, rows, index_ref, left_ref, right_ref, *refs):
    extra_ref = refs[0] if len(refs) > count + 1 else None
    outs, held_ref = refs[-1 - count : -1], refs[-1]
    width = right_ref.shape[1]
    held_ref[...] = left_inner(left_ref[...], right_ref[...]).astype(BF)
    for i in range(count):
        for part in range(outer):
            source = pl.ds(pl.multiple_of((part * count + index_ref[i]) * rows, 16), rows)
            outs[i][part, :, :width] = held_ref[source, :]
            if extra_ref is not None:
                outs[i][part, :, width:] = extra_ref[source, :]


def weight_grad(left, right, extra, index, count, rows):
    outer = left.shape[1] // (count * rows)
    arrays = [left, right] + ([] if extra is None else [extra])
    if rows % 16:
        wide = left_inner(left, right).astype(BF)
        wide = wide if extra is None else jnp.concatenate([wide, extra], 1)
        return take([wide.reshape(outer, count, rows, -1)], index)
    width = sum(array.shape[1] for array in arrays[1:])
    return pl.pallas_call(
        functools.partial(weight_grad_kernel, outer, count, rows),
        grid_spec=pltpu.PrefetchScalarGridSpec(
            num_scalar_prefetch=1,
            grid=(1,),
            in_specs=[pl.BlockSpec(array.shape, lambda p, *_: (0, 0)) for array in arrays],
            out_specs=[pl.BlockSpec((outer, rows, width), lambda p, *_: (0, 0, 0))] * count,
            scratch_shapes=[pltpu.VMEM((left.shape[1], right.shape[1]), BF)],
        ),
        out_shape=[jax.ShapeDtypeStruct((outer, rows, width), BF)] * count,
        cost_estimate=BRIEF,
        name="weight_grad",
    )(index, *arrays)


def hidden_back_kernel(own_steps, rows_ref, down_ref, slope_ref, up_ref, grad_ref, own_ref, other_ref):
    grad = (times_transposed(rows_ref[...], down_ref[...]) * slope_ref[...]).astype(BF)
    grad_ref[...] = grad
    partial = times_transposed(grad, up_ref[...])

    @pl.when(pl.program_id(0) < own_steps)
    def _():
        own_ref[...] = partial

    @pl.when(pl.program_id(0) >= own_steps)
    def _():
        other_ref[...] = partial.astype(BF)


def hidden_back(rows, down, slope, up):
    total, width = rows.shape
    units = slope.shape[1]
    block = 256 if total % 512 == 0 else total // 2
    own_steps = total // 2 // block
    return pl.pallas_call(
        functools.partial(hidden_back_kernel, own_steps),
        grid=(total // block,),
        in_specs=[
            pl.BlockSpec((block, width), lambda i: (i, 0)),
            pl.BlockSpec((units, width), lambda i: (0, 0), pipeline_mode=pl.Buffered(1)),
            pl.BlockSpec((block, units), lambda i: (i, 0)),
            pl.BlockSpec((width, units), lambda i: (0, 0), pipeline_mode=pl.Buffered(1)),
        ],
        out_specs=[
            pl.BlockSpec((block, units), lambda i: (i, 0)),
            pl.BlockSpec((block, width), lambda i: (jnp.minimum(i, own_steps - 1), 0)),
            pl.BlockSpec((block, width), lambda i: (jnp.maximum(i - own_steps, 0), 0)),
        ],
        out_shape=[
            jax.ShapeDtypeStruct((total, units), BF),
            jax.ShapeDtypeStruct((total // 2, width), F32),
            jax.ShapeDtypeStruct((total // 2, width), BF),
        ],
        cost_estimate=BRIEF,
        name="hidden_back",
    )(rows, down, slope, up)


def sum_take_kernel(count, index_ref, *refs):
    arrays, outs = refs[:-count], refs[-count:]
    for i in range(count):
        total = arrays[0][:, index_ref[i]].astype(F32)
        for array in arrays[1:]:
            total += array[:, index_ref[i]].astype(F32)
        outs[i][...] = total.astype(BF)


def sum_take(arrays, index, count):
    arrays = [array.reshape((-1, count) + array.shape[1:]) for array in arrays]
    outer, _, rows, width = arrays[0].shape
    return pl.pallas_call(
        functools.partial(sum_take_kernel, count),
        grid_spec=pltpu.PrefetchScalarGridSpec(
            num_scalar_prefetch=1,
            grid=(1,),
            in_specs=[pl.BlockSpec(array.shape, lambda p, *_: (0, 0, 0, 0)) for array in arrays],
            out_specs=[pl.BlockSpec((outer, rows, width), lambda p, *_: (0, 0, 0))] * count,
        ),
        out_shape=[jax.ShapeDtypeStruct((outer, rows, width), BF)] * count,
        cost_estimate=BRIEF,
        name="sum_take",
    )(index, *arrays)


class Links:
    def __init__(self, mesh):
        self.devices = mesh.shape["wide"] * mesh.shape["narrow"]
        self.chips = self.devices // 2
        bits = self.chips.bit_length() - 1
        assert self.chips == 1 << bits
        self.groups = [(low, 2) for low in range(bits - 2, -1, -2)]
        if bits % 2:
            self.groups.append((0, 1))
        self.own = lax.axis_index(AXES)
        self.chip = self.own // 2
        self.core = self.own % 2

    def send(self, value, flip_even, flip_odd):
        pairs = [(d, d ^ (flip_odd if d % 2 else flip_even)) for d in range(self.devices)]
        return lax.ppermute(value, AXES, pairs)

    def core_swap(self, value):
        return self.send(value, 1, 1)

    def row_swap(self, value):
        return self.send(value, 2, 2)

    def spots(self, low, size):
        place = (self.chip >> low) % (1 << size)
        if size == 1:
            return jnp.stack([place, place ^ 1]).astype(jnp.int32)
        first, second = 1 + self.core, 2 - self.core
        return jnp.stack([place, place ^ first, place ^ second, place ^ 3]).astype(jnp.int32)

    def gather(self, block, high, columns=None):
        width = block.shape[1]
        have = block[None]
        groups = self.groups if high else self.groups[::-1]
        for stage, (low, size) in enumerate(groups):
            if size == 1:
                (one,) = yield (self.send(have, 2 << low, 2 << low),)
                yield ()
                pieces = [have, one]
            else:
                one = self.send(have, 2 << low, 4 << low)
                two = self.send(have, 4 << low, 2 << low)
                one, two = yield (one, two)
                (three,) = yield (self.send(one, 4 << low, 2 << low),)
                pieces = [have, one, two, three]
            last = stage == len(groups) - 1
            placed = place(pieces, self.spots(low, size), columns if last and columns else ((0, width),))
            if high:
                placed = [out.reshape((-1,) + out.shape[2:]) for out in placed]
            else:
                placed = [out.reshape(1, -1, out.shape[3]) for out in placed]
            placed = yield tuple(placed)
            have = placed[0]

    def scatter(self, left, right, extra=None):
        rows = left.shape[1] // self.chips
        for stage, (low, size) in enumerate(self.groups[::-1]):
            spots, count = self.spots(low, size), 1 << size
            if stage:
                pieces = sum_take(parts, spots, count)
            else:
                pieces = weight_grad(left, right, extra, spots, count, rows)
            pieces = yield tuple(pieces)
            if size == 1:
                (got,) = yield (self.send(pieces[1], 2 << low, 2 << low),)
                yield ()
                parts = [pieces[0], got]
            else:
                three = self.send(pieces[3], 4 << low, 2 << low)
                two = self.send(pieces[2], 4 << low, 2 << low)
                three, two = yield (three, two)
                one = (pieces[1].astype(F32) + three.astype(F32)).astype(BF)
                (one,) = yield (self.send(one, 2 << low, 4 << low),)
                parts = [pieces[0], two, one]
        yield (sum(part[0].astype(F32) for part in parts),)


class Flow:
    def __init__(self, steps):
        self.steps = steps
        self.pending = next(steps)
        self.running = True

    def go(self, values):
        try:
            self.pending = self.steps.send(values)
        except StopIteration:
            self.pending = values
            self.running = False


def release(*flows, ties=()):
    held = lax.optimization_barrier((tuple(flow.pending for flow in flows), ties))
    for flow, values in zip(flows, held[0]):
        flow.go(values)
    return held[1]


def finish(flow):
    while flow.running:
        release(flow)
    return flow.pending


def after(value, others):
    return lax.optimization_barrier((value, others))[0]


def pick(parts, at, axis):
    return lax.dynamic_index_in_dim(parts, at, axis, keepdims=False)


def by_core(core, own, other, axis):
    return jnp.where(
        core == 0, jnp.concatenate([own, other], axis), jnp.concatenate([other, own], axis)
    )


def normalize(rows):
    average = jnp.mean(rows, -1, keepdims=True)
    centered = rows - average
    scale = lax.rsqrt(jnp.mean(centered * centered, -1, keepdims=True) + EPS)
    return centered * scale, scale


def normalize_back(grads, normal, scale):
    return (
        grads
        - jnp.mean(grads, -1, keepdims=True)
        - normal * jnp.mean(grads * normal, -1, keepdims=True)
    ) * scale


def local(mesh):
    def run(
        layer_in, doc_ids, in_proj, out_proj, vec_bias, norm_gain, ffn_in, ffn_bias, ffn_out, out_grad
    ):
        links = Links(mesh)
        core, chips = links.core, links.chips
        side = (links.own // 2) % 2
        slots, shard, _ = layer_in.shape
        assert slots == 2 and mesh.shape["narrow"] == 4
        own_rows = in_proj.shape[1]
        chip_rows = 2 * own_rows
        hidden = ffn_out.shape[0]

        def halves(array):
            left, right = jnp.split(array, 2, -1)
            return jnp.where(core == 0, left, right), jnp.where(core == 0, right, left)

        keep = pick(layer_in, side, 0)
        got_tokens = links.row_swap(pick(layer_in, 1 - side, 0))

        split = 3 * HALF
        trio_mine, trio_other = halves(in_proj)
        vectors = jnp.pad(jnp.concatenate([vec_bias, norm_gain], 0).T, ((0, 0), (0, SMALL - 8)))
        mine = jnp.concatenate([trio_mine[0], trio_mine[1], trio_mine[2], vectors], 1)
        other = jnp.concatenate([trio_other[0], trio_other[1], trio_other[2], vectors], 1)
        cols = by_core(core, mine, links.core_swap(other), 0)
        small = jnp.concatenate(
            [
                cols[:, split : split + 8],
                ffn_bias.reshape(chip_rows, 2),
                jnp.zeros((chip_rows, SMALL - 10), BF),
            ],
            1,
        )
        attn_block = jnp.concatenate([cols[:, :split], small], 1)
        attn = Flow(links.gather(attn_block, True, ((0, split), (split, split + SMALL))))
        down = Flow(links.gather(ffn_out, False))
        (got_tokens,) = release(attn, down, ties=(got_tokens,))
        tokens = jnp.concatenate([keep, got_tokens], 0)
        release(attn, down)
        release(attn)
        release(down)

        ffn_cols = ffn_in.reshape(own_rows, chips, 2, hidden).transpose(0, 2, 1, 3)
        ffn_cols = ffn_cols.reshape(own_rows, 2, chips * hidden)
        out_mine, out_other = halves(out_proj)
        mine = jnp.concatenate([pick(ffn_cols, core, 1), out_mine], 1)
        other = jnp.concatenate([pick(ffn_cols, 1 - core, 1), out_other], 1)
        cols = by_core(core, mine, links.core_swap(other), 0)
        up = Flow(links.gather(cols, True, ((0, FF // 2), (FF // 2, FF // 2 + HALF))))
        all_tokens = jnp.concatenate([tokens, links.core_swap(tokens)], 0)
        release(attn, up)
        (all_tokens,) = release(attn, up, ties=(all_tokens,))
        (all_tokens,) = release(up, ties=(all_tokens,))
        attn_pack = finish(attn)
        trio_weight = attn_pack[0].reshape(D, split)
        small = attn_pack[1]
        bias = small[..., :8].reshape(D, 8).T.astype(F32)
        up_bias = small[..., 8:10].reshape(FF // 2).astype(F32)

        slot_ids = pick(doc_ids, side, 0).reshape(2, 2, shard)
        slot_ids = jnp.stack(
            [
                slot_ids[side, core],
                slot_ids[1 - side, core],
                slot_ids[side, 1 - core],
                slot_ids[1 - side, 1 - core],
            ]
        )
        id_col = slot_ids.reshape(-1, 1)
        id_row = slot_ids.reshape(1, -1)
        low, high = jnp.min(slot_ids, 1), jnp.max(slot_ids, 1)

        own_bias = pick(bias[:2].reshape(2, 2, HALF), core, 1)
        zero = jnp.zeros_like(own_bias[0])
        trio_bias = jnp.concatenate([own_bias[0], zero, own_bias[1]])
        trio_scale = jnp.concatenate([zero + 0.125, zero + 1.0, zero + 1.0])
        trios = ((matmul(all_tokens, trio_weight) + trio_bias) * trio_scale).astype(BF)
        trios, row_grads = release(up, down, ties=(trios, out_grad))
        got_grads = links.row_swap(pick(row_grads, 1 - side, 0))
        mixed_heads, lse = attend(trios, low, high, id_col, id_row)
        mixed_heads, got_grads = release(up, down, ties=(mixed_heads, got_grads))
        grad_out = jnp.concatenate([pick(row_grads, side, 0), got_grads], 0).astype(F32)
        up_weight, out_half = finish(up)
        down_weight = finish(down)[0][0]
        up_weight = up_weight.reshape(D, FF // 2)
        out_half = out_half.reshape(D, HALF)
        out_weight = by_core(core, out_half, links.core_swap(out_half), 1)
        count = tokens.shape[0]
        mixed = by_core(core, mixed_heads[:count], links.core_swap(mixed_heads[count:]), 1)

        first_sum = tokens.astype(F32) + matmul(mixed, out_weight) + bias[2]
        first_normal, first_scale = normalize(first_sum)
        normed = first_normal * bias[6] + bias[3]
        normed_low = normed.astype(BF)
        all_normed = lax.optimization_barrier(
            jnp.concatenate([normed_low, links.core_swap(normed_low)], 0)
        )
        upper = matmul(all_normed, up_weight) + up_bias
        erf_part = 1.0 + lax.erf(upper * 0.7071067811865476)
        active = (0.5 * upper * erf_part).astype(BF)
        slope = 0.5 * erf_part + upper * jnp.exp(-0.5 * upper * upper) * 0.3989422804014327
        active, slope = lax.optimization_barrier((active, slope))
        partial = matmul(active, down_weight)
        second_sum = (
            normed
            + partial[:count]
            + links.core_swap(partial[count:].astype(BF)).astype(F32)
            + bias[4]
        )
        second_normal, second_scale = normalize(second_sum)
        result = (second_normal * bias[7] + bias[5]).astype(BF)

        def home(rows, got):
            kept = rows[:shard]
            return jnp.stack([jnp.where(side == 0, kept, got), jnp.where(side == 0, got, kept)])

        got_result = links.row_swap(result[shard:])

        grad_second = normalize_back(grad_out * bias[7], second_normal, second_scale)
        grad_down = grad_second.astype(BF)
        all_down = lax.optimization_barrier(
            jnp.concatenate([grad_down, links.core_swap(grad_down)], 0)
        )
        grad_upper, partial, partial_other = hidden_back(all_down, down_weight, slope, up_weight)
        down_sum = Flow(links.scatter(active, all_down))
        (partial_got,) = release(down_sum, ties=(links.core_swap(partial_other),))
        grad_normed = grad_second + partial + partial_got.astype(F32)
        grad_first = normalize_back(grad_normed * bias[6], first_normal, first_scale)
        grad_attn = grad_first.astype(BF)
        grad_out_weight = left_inner(mixed, grad_attn).astype(BF)
        grad_mixed = times_transposed(grad_attn, out_weight).astype(BF)
        mine, other = halves(grad_mixed)
        grad_heads = jnp.concatenate([mine, links.core_swap(other)], 0)
        mine, other = halves(grad_out_weight)
        out_sum = (mine.astype(F32) + links.core_swap(other).astype(F32)).astype(BF)
        up_sum = Flow(links.scatter(all_normed, grad_upper, out_sum))
        (grad_heads,) = release(down_sum, up_sum, ties=(grad_heads,))
        grad_trios, trio_sums = attend_back(
            trios, grad_heads, mixed_heads, low, high, id_col, id_row, lse
        )
        trio_sums = trio_sums[0].reshape(3, HALF)

        own_half = jnp.stack([trio_sums[0], trio_sums[2]])
        none = jnp.zeros_like(own_half)
        sums = jnp.concatenate(
            [
                by_core(core, own_half, none, 1),
                jnp.stack(
                    [
                        jnp.sum(grad_attn.astype(F32), 0),
                        jnp.sum(grad_normed, 0),
                        jnp.sum(grad_down.astype(F32), 0),
                        jnp.sum(grad_out, 0),
                        jnp.sum(grad_normed * first_normal, 0),
                        jnp.sum(grad_out * second_normal, 0),
                    ]
                ),
            ],
            0,
        )
        up_bias_sum = jnp.sum(grad_upper.astype(F32), 0).reshape(D, 2)
        small = jnp.concatenate(
            [sums.T, up_bias_sum, jnp.zeros((D, SMALL - 10), F32)], 1
        ).astype(BF)
        attn_sum = Flow(links.scatter(all_tokens, grad_trios, small))
        grad_trios, got_result = release(
            attn_sum, down_sum, up_sum, ties=(grad_trios, got_result)
        )
        layer_out = home(result, got_result)
        partial = times_transposed(grad_trios, trio_weight)
        grad_tokens = (
            grad_first
            + partial[:count]
            + links.core_swap(partial[count:].astype(BF)).astype(F32)
        )
        grad_tokens = grad_tokens.astype(BF)
        grad_in = home(grad_tokens, links.row_swap(grad_tokens[shard:]))

        release(up_sum, down_sum)
        release(attn_sum, up_sum)
        release(attn_sum, up_sum)
        release(attn_sum)
        release(attn_sum, up_sum, down_sum)
        down_total = finish(down_sum)[0]
        up_total = finish(up_sum)[0]
        attn_total = finish(attn_sum)[0]

        def both(array):
            rows = array.reshape(2, own_rows, -1)
            other = links.core_swap(pick(rows, 1 - core, 0).astype(BF))
            return pick(rows, core, 0), other.astype(F32)

        mine, got = both(up_total)
        grad_ffn_in = by_core(
            core,
            mine[:, : FF // 2].reshape(own_rows, chips, 1, hidden),
            got[:, : FF // 2].reshape(own_rows, chips, 1, hidden),
            2,
        ).reshape(own_rows, FF)
        grad_out_proj = by_core(core, mine[:, FF // 2 :], got[:, FF // 2 :], 1)
        mine, got = both(attn_total)
        grad_in_proj = jnp.stack(
            [
                by_core(core, mine[:, i * HALF : (i + 1) * HALF], got[:, i * HALF : (i + 1) * HALF], 1)
                for i in range(3)
            ]
        )
        vectors = (mine[:, split : split + 8] + got[:, split : split + 8]).T
        grad_ffn_bias = attn_total[:, split + 8 : split + 10].reshape(hidden)
        return (
            layer_out,
            grad_in,
            grad_in_proj,
            grad_out_proj,
            vectors[:6],
            vectors[6:],
            grad_ffn_in,
            grad_ffn_bias,
            down_total,
        )

    return run


def solution(mesh):
    return jax.shard_map(
        local(mesh),
        mesh=mesh,
        in_specs=(
            P("wide", "narrow", None),
            P("wide", None),
            P(None, AXES, None),
            P(AXES, None),
            P(None, AXES),
            P(None, AXES),
            P(AXES, None),
            P(AXES),
            P(AXES, None),
            P("wide", "narrow", None),
        ),
        out_specs=(
            P("wide", "narrow", None),
            P("wide", "narrow", None),
            P(None, AXES, None),
            P(AXES, None),
            P(None, AXES),
            P(None, AXES),
            P(AXES, None),
            P(AXES),
            P(AXES, None),
        ),
        check_vma=False,
    )
```
